32 devices in a mesh: gx: 8 (over z, core), gy: 4 (over y, x).
Axes of the slice: x: 2, y: 2, z: 4, core: 2. Of those that a mesh axis runs over, the one named last changes fastest.
Arguments:
- basis: float32 [8, 4, 96, 2048], P('gx', 'gy')
- block_vals: float32 [8, 4, 16, 5, 128, 128], P('gx', 'gy'), as said below
- block_cols: int32 [8, 4, 16, 5], P('gx', 'gy'), may hold values from 0 to 15, as said below
- edge_rows: int32 [8, 4, 4, 256], P('gx', 'gy'), may hold values from 0 to 2047, as said below
- live_counts: int32 [8, 4], P('gx', 'gy'), may hold values from 1024 to 2048, as said below
Outputs:
- encoding: float32 [8, 4, 96, 2048], P('gx', 'gy')
The draws below stay inside these ranges and needn't reach their ends.
Inputs may be any that keep to these rules, and one draw needn't show every extreme that they name: `live_counts`: every tile has 1024 or more live cells, and some tile is full. `block_cols`: entries name blocks of the same tile. `block_vals`: weights are nonnegative; the weight between two cells is the same in both stored blocks that hold it, and a cell has no weight to itself. `edge_rows`: every entry is a live cell of its tile.
All inputs are finite; a program needn't handle non-finite values.
Results may differ from the reference program's by a relative error of at most 0.0001.
Values sent between devices are 32-bit elements; how exact they have to be, the bound alone decides.
No kernel may reach another device: no remote copies, remote signals or barrier semaphores. Data moves between devices by JAX's collectives and lax.ppermute only.
A program may use at most 64 MiB of HBM per device.

```python
import math
import jax
import jax.numpy as jnp
from jax import lax

K = 96
BLK = 128
NB = 16
NNZB = 5
HB = 256
DEGREE = 4
CELLS_DEV = 2048
TOTAL_CELLS = 65536
N_GX = 8
N_GY = 4


def tile_offsets(key):
    key_score = jax.random.fold_in(key, 11)
    choices_count = NB // 2 - 1
    scores = jax.random.randint(key_score, (N_GX, N_GY, choices_count), 0, 1 << 20) * choices_count
    scores = scores + lax.iota(jnp.int32, choices_count)[None, None, :]
    order = jnp.argsort(scores, axis=-1, stable=True).astype(jnp.int32)
    return (order[:, :, 0] + 1, order[:, :, 1] + 1)


def tile_counts(key):
    key_raw, key_full = jax.random.split(jax.random.fold_in(key, 23))
    raw_counts = jax.random.randint(key_raw, (N_GX * N_GY,), CELLS_DEV // 2, CELLS_DEV + 1)
    full_tile = jax.random.randint(key_full, (), 0, N_GX * N_GY)
    raw_counts = jnp.where(jnp.arange(N_GX * N_GY, dtype=jnp.int32) == full_tile, CELLS_DEV, raw_counts)
    return raw_counts.reshape(N_GX, N_GY).astype(jnp.int32)


def shifted_blocks(stack_blocks, offsets):
    source = (lax.iota(jnp.int32, NB)[None, :] - offsets.reshape(-1)[:, None]) % NB
    return jnp.take_along_axis(stack_blocks, source[:, :, None, None], axis=1)


def draw_live_counts(key, part):
    return tile_counts(key)


def draw_block_cols(key, part):
    first, second = tile_offsets(key)
    zeros_shift = jnp.zeros_like(first)
    shifts = jnp.stack([zeros_shift, first, -first, second, -second], -1)[:, :, None, :]
    base_rows = lax.iota(jnp.int32, NB)[None, None, :, None]
    return ((base_rows + shifts) % NB).astype(jnp.int32)


def draw_edge_rows(key, part):
    counts = tile_counts(key)
    key_rows, key_place = jax.random.split(jax.random.fold_in(key, 53))
    raw_rows = jax.random.randint(key_rows, (N_GX, N_GY, 4 * HB), 0, counts[:, :, None])
    place = jax.random.randint(key_place, (N_GX, N_GY, 1), 0, 4 * HB)
    raw_rows = jnp.where(lax.iota(jnp.int32, 4 * HB)[None, None, :] == place, counts[:, :, None] - 1, raw_rows)
    return raw_rows.reshape(N_GX, N_GY, 4, HB).astype(jnp.int32)


def draw_block_vals(key, part):
    first, second = tile_offsets(key)
    key_size, key_keep = jax.random.split(jax.random.fold_in(key, 37))
    shape = (N_GX * N_GY, NB, 3, BLK, BLK)
    magnitude = jax.random.uniform(key_size, shape, jnp.float32, 0.5, 1.5)
    growth = 3.0
    raw_weights = magnitude * jax.random.bernoulli(key_keep, 0.25, shape).astype(jnp.float32)
    own_block = raw_weights[:, :, 0]
    own_block = 0.5 * (own_block + jnp.swapaxes(own_block, -1, -2)) * (1.0 - jnp.eye(BLK, dtype=jnp.float32))
    forward_first = raw_weights[:, :, 1]
    forward_second = raw_weights[:, :, 2]
    back_first = jnp.swapaxes(shifted_blocks(forward_first, first), -1, -2)
    back_second = jnp.swapaxes(shifted_blocks(forward_second, second), -1, -2)
    stacked = jnp.stack([own_block, forward_first, back_first, forward_second, back_second], axis=2)
    row_place = lax.iota(jnp.float32, N_GX) / max(N_GX - 1, 1)
    col_place = lax.iota(jnp.float32, N_GY) / max(N_GY - 1, 1)
    density = (growth ** (0.5 * (row_place[:, None] + col_place[None, :]))).reshape(-1) / 40.0
    stacked = stacked * density[:, None, None, None, None]
    return stacked.reshape(N_GX, N_GY, NB, NNZB, BLK, BLK)


def draw_basis(key, part):
    key_base, key_cols, key_rows = jax.random.split(jax.random.fold_in(key, 41), 3)
    shape = (N_GX, N_GY, K, CELLS_DEV)
    column_scale = jnp.exp(jax.random.uniform(key_cols, (K,), jnp.float32, 0.0, math.log(10.0)))
    row_scale = jnp.exp(jax.random.uniform(key_rows, (N_GX, N_GY, 1, CELLS_DEV), jnp.float32, 0.0, math.log(10.0)))
    base_values = jax.random.normal(key_base, shape, jnp.float32)
    return base_values * column_scale[None, None, :, None] * row_scale


def setup_inputs(seed: int = 0) -> dict:
    key_list = jax.random.split(jax.random.key(seed), 6)
    basis = draw_basis(jax.random.fold_in(key_list[5], 71), 0)
    block_vals = draw_block_vals(jax.random.fold_in(key_list[5], 71), 0)
    block_cols = draw_block_cols(jax.random.fold_in(key_list[5], 71), 0)
    edge_rows = draw_edge_rows(jax.random.fold_in(key_list[5], 71), 0)
    live_counts = draw_live_counts(jax.random.fold_in(key_list[5], 71), 0)
    return {"basis": basis, "block_vals": block_vals, "block_cols": block_cols, "edge_rows": edge_rows, "live_counts": live_counts}


PRECISE = lax.Precision.HIGHEST
LOWER_FRACTION = 0.125

def block_product(tile_weights, tile_columns, values):
    vec_count = values.shape[0]
    block_view = values.reshape(vec_count, NB, BLK)
    picked_blocks = jnp.take(block_view, tile_columns.reshape(-1), axis=1).reshape(vec_count, NB, NNZB, BLK)
    product = jnp.einsum('knjc,njrc->knr', picked_blocks, tile_weights, precision=PRECISE)
    return product.reshape(vec_count, NB * BLK)

def reference(basis, block_vals, block_cols, edge_rows, live_counts):
    tile_count = N_GX * N_GY
    weights = block_vals.reshape(tile_count, NB, NNZB, BLK, BLK)
    columns = block_cols.reshape(tile_count, NB, NNZB)
    edge_lists = edge_rows.reshape(tile_count, 4 * HB)
    live_mask = (lax.iota(jnp.int32, CELLS_DEV)[None, :] < live_counts.reshape(tile_count, 1)).astype(jnp.float32)
    tile_row = jnp.arange(N_GX, dtype=jnp.int32)[:, None] * jnp.ones((1, N_GY), jnp.int32)
    tile_col = jnp.ones((N_GX, 1), jnp.int32) * jnp.arange(N_GY, dtype=jnp.int32)[None, :]
    has_neighbour = jnp.stack([tile_row > 0, tile_row < N_GX - 1, tile_col > 0, tile_col < N_GY - 1], -1)
    has_neighbour = has_neighbour.astype(jnp.float32).reshape(tile_count, 4)

    def count_edges(tile_lists, tile_flags):
        return jnp.zeros((CELLS_DEV,), jnp.float32).at[tile_lists].add(jnp.repeat(tile_flags, HB))
    cross_count = jax.vmap(count_edges)(edge_lists, has_neighbour)

    def mask_sum(packed):
        return block_product(packed[0], packed[1], packed[2][None])[0]
    own_sum = lax.map(mask_sum, (weights, columns, live_mask))
    degree = live_mask * (own_sum + cross_count)
    upper_bound = 2.0 * jnp.max(degree)

    def take_edges(values, tile_lists):
        return jnp.take(values, tile_lists, axis=1)

    def add_edges(tile_lists, incoming):
        return jnp.zeros((K, CELLS_DEV), jnp.float32).at[:, tile_lists].add(incoming)

    def crossing(values):
        outgoing = jax.vmap(take_edges)(values, edge_lists).reshape(N_GX, N_GY, K, 4, HB)
        zero_row = jnp.zeros_like(outgoing[:1, :, :, 0])
        zero_col = jnp.zeros_like(outgoing[:, :1, :, 0])
        from_low_x = jnp.concatenate([zero_row, outgoing[:-1, :, :, 1]], 0)
        from_high_x = jnp.concatenate([outgoing[1:, :, :, 0], zero_row], 0)
        from_low_y = jnp.concatenate([zero_col, outgoing[:, :-1, :, 3]], 1)
        from_high_y = jnp.concatenate([outgoing[:, 1:, :, 2], zero_col], 1)
        incoming = jnp.stack([from_low_x, from_high_x, from_low_y, from_high_y], 3).reshape(tile_count, K, 4 * HB)
        return jax.vmap(add_edges)(edge_lists, incoming)

    def local_part(packed):
        return block_product(packed[0], packed[1], packed[2])

    def operator(values):
        inside = lax.map(local_part, (weights, columns, values))
        return live_mask[:, None, :] * (degree[:, None, :] * values - inside - crossing(values))
    lower_edge = LOWER_FRACTION * upper_bound
    half_width = (upper_bound - lower_edge) / 2.0
    centre = (upper_bound + lower_edge) / 2.0
    previous = live_mask[:, None, :] * basis.reshape(tile_count, K, CELLS_DEV)
    current = (operator(previous) - centre * previous) / half_width
    for repeat in range(DEGREE - 1):
        following = 2.0 / half_width * (operator(current) - centre * current) - previous
        previous = current
        current = following
    gram = jnp.einsum('tkc,tlc->kl', current, current, precision=PRECISE)
    factor_lower = jnp.linalg.cholesky(gram)
    inverse = jax.scipy.linalg.solve_triangular(factor_lower, jnp.eye(K, dtype=jnp.float32), lower=True)
    encoding = jnp.einsum('kl,tlc->tkc', inverse, current, precision=PRECISE) * math.sqrt(TOTAL_CELLS)
    return encoding.reshape(N_GX, N_GY, K, CELLS_DEV)
```

```python
import functools
import math

import jax
import jax.numpy as jnp
from jax import lax
from jax.experimental import pallas as pl
from jax.experimental.pallas import tpu as pltpu
from jax.sharding import PartitionSpec as P

DEGREE = 4
LOWER_FRACTION = 0.125
LANES = 128
CHUNK = 256
F32 = jnp.float32
BF16 = jnp.bfloat16
NT = (((1,), (1,)), ((), ()))
VM = pl.BlockSpec(memory_space=pltpu.VMEM)
SM = pl.BlockSpec(memory_space=pltpu.SMEM)
LIMIT = 40 << 20


def split(x):
    hi = x.astype(BF16)
    return hi, (x - hi.astype(F32)).astype(BF16)


def stacked(x):
    return jnp.concatenate(split(x), axis=0)


def folded(x):
    half = x.shape[0] // 2
    return x[:half] + x[half:]


def dot(a, b):
    return jnp.dot(a, b, preferred_element_type=F32)


def swap_lists(size, shift):
    pairs = []
    for low in range(shift, size - 1, 2):
        pairs += [(low, low + 1), (low + 1, low)]
    return pairs


def xor_pairs(size, bit):
    return [(i, i ^ bit) for i in range(size)]


def live_lanes(count, start, width):
    return lax.broadcasted_iota(jnp.int32, (1, width), 1) + start < count


def edges_kernel(counts, lists, basis, place, *outs):
    cells, edges = place.shape
    rows = lists[0, 0]
    odd = [lax.axis_index(axis) % 2 for axis in ("gx", "gy")]
    row = lambda i: rows[i : i + 1]
    order = []
    for dim, flag in enumerate(odd):
        low, high = row(2 * dim), row(2 * dim + 1)
        order += [jnp.where(flag == 1, low, high), jnp.where(flag == 1, high, low)]
    targets = jnp.concatenate(order, axis=1)
    for start in range(0, cells, CHUNK):
        spot = lax.broadcasted_iota(jnp.int32, (CHUNK, edges), 0) + start
        place[start : start + CHUNK] = (spot == targets).astype(F32).astype(BF16)
    picked = folded(dot(stacked(basis[0, 0]), place[...]))
    width = edges // len(outs)
    for i, out in enumerate(outs):
        out[...] = picked[:, i * width : (i + 1) * width]


def first_product_kernel(sizes, counts, cols, weights, basis, place, stored, inside, degree, peak, total):
    step = pl.program_id(0)
    vecs = inside.shape[0]
    slots = weights.shape[3]
    count = counts[0, 0]

    @pl.when(step == 0)
    def _():
        total[...] = jnp.zeros_like(total)

    for j in range(slots):
        hi, lo = split(weights[0, 0, 0, j])
        stored[step, 0:LANES, j * LANES : (j + 1) * LANES] = hi
        stored[step, LANES : 2 * LANES, j * LANES : (j + 1) * LANES] = lo
    start = pl.multiple_of(step * LANES, LANES)
    live = live_lanes(count, start, LANES)
    hi, lo = split(jnp.where(live, basis[0, 0, :, pl.ds(start, LANES)], 0.0))
    ones = jnp.broadcast_to(live.astype(F32), (16, LANES)).astype(BF16)
    left = jnp.concatenate(
        [
            jnp.concatenate([hi, hi], axis=1),
            jnp.concatenate([lo, jnp.zeros_like(lo)], axis=1),
            jnp.concatenate([ones, ones], axis=1),
        ],
        axis=0,
    )
    product = dot(left, stored[step])
    product = jnp.concatenate(
        [product[:vecs] + product[vecs : 2 * vecs], product[2 * vecs : 2 * vecs + 8]], axis=0
    )
    for j in range(slots):
        spot = pl.ds(pl.multiple_of(cols[0, 0, step, j] * LANES, LANES), LANES)
        total[:, spot] += product[:, j * LANES : (j + 1) * LANES]

    @pl.when(step == pl.num_programs(0) - 1)
    def _():
        cells, edges = place.shape
        width = edges // 4
        flags = []
        for axis, size in zip(("gx", "gy"), sizes):
            me = lax.axis_index(axis)
            odd = me % 2
            for mate in (me + 1 - 2 * odd, me - 1 + 2 * odd):
                here = jnp.logical_and(mate >= 0, mate < size).astype(F32)
                flags.append(jnp.full((16, width), here, F32))
        known = jnp.concatenate(flags, axis=1).astype(BF16)
        joined = lax.dot_general(known, place[...], NT, preferred_element_type=F32)[:8]
        inside[...] = total[:vecs]
        value = jnp.where(live_lanes(count, 0, cells), total[vecs : vecs + 8] + joined, 0.0)
        degree[...] = value
        peak[...] = jnp.full(peak.shape, jnp.max(value), F32)


def product_kernel(cols, values, stored, inside):
    blocks, _, width = stored.shape
    inside[...] = jnp.zeros_like(inside)
    for m in range(blocks):
        hi, lo = split(values[:, m * LANES : (m + 1) * LANES])
        left = jnp.concatenate(
            [
                jnp.concatenate([hi, hi], axis=1),
                jnp.concatenate([lo, jnp.zeros_like(lo)], axis=1),
            ],
            axis=0,
        )
        product = folded(dot(left, stored[m]))
        for j in range(width // LANES):
            spot = pl.ds(pl.multiple_of(cols[0, 0, m, j] * LANES, LANES), LANES)
            inside[:, spot] += product[:, j * LANES : (j + 1) * LANES]


def combine_kernel(number, counts, r0, r1, r2, r3, inside, current, previous, degree, peak, place, following, *outs):
    cells, edges = place.shape
    count = counts[0, 0]
    upper = 2.0 * peak[0:1, 0:1]
    lower = LOWER_FRACTION * upper
    half = (upper - lower) / 2.0
    centre = (upper + lower) / 2.0
    scale = (1.0 if number == 0 else 2.0) / half
    arrived = stacked(jnp.concatenate([r0[...], r1[...], r2[...], r3[...]], axis=1))
    for start in range(0, cells, CHUNK):
        part = slice(start, start + CHUNK)
        crossed = folded(
            lax.dot_general(arrived, place[part], NT, preferred_element_type=F32)
        )
        live = live_lanes(count, start, CHUNK)
        now = current[0, 0, :, part] if number == 0 else current[:, part]
        if number == 0:
            now = jnp.where(live, now, 0.0)
        value = (degree[0:1, part] - centre) * now
        value = scale * (value - jnp.where(live, inside[:, part] + crossed, 0.0))
        if number > 0:
            before = previous[0, 0, :, part] if number == 1 else previous[:, part]
            if number == 1:
                before = jnp.where(live, before, 0.0)
            value = value - before
        following[:, part] = value
    if len(outs) == 1:
        whole = following[...]
        outs[0][...] = lax.dot_general(
            whole, whole, NT, precision=lax.Precision.HIGHEST, preferred_element_type=F32
        )
    else:
        picked = folded(dot(stacked(following[...]), place[...]))
        width = edges // len(outs)
        for i, out in enumerate(outs):
            out[...] = picked[:, i * width : (i + 1) * width]


def encode_kernel(root, first, second, values, out):
    gram = first[...] + second[...]
    vecs = gram.shape[0]
    lane = lax.broadcasted_iota(jnp.int32, (8, vecs), 1)
    sub = lax.broadcasted_iota(jnp.int32, (8, vecs), 0)
    rows = [gram[i * 8 : i * 8 + 8] for i in range(vecs // 8)]
    for k in range(vecs):
        g, r = divmod(k, 8)
        pivot = jnp.broadcast_to(rows[g][r : r + 1], (8, vecs))
        inverse = 1.0 / jnp.broadcast_to(rows[g][r : r + 1, k : k + 1], (8, vecs))
        step_row = jnp.where(lane == k, 1.0, pivot)
        for i in range(g, vecs // 8):
            factor = jnp.broadcast_to(rows[i][:, k : k + 1], (8, vecs)) * inverse
            kept = jnp.where(lane == k, 0.0, rows[i])
            done = kept - factor * step_row
            if i == g:
                scaled = lax.rsqrt(pivot[:, k : k + 1]) * jnp.where(lane == k, 1.0, jnp.where(lane < k, pivot, 0.0))
                done = jnp.where(sub > r, done, jnp.where(sub == r, scaled, rows[i]))
            rows[i] = done
    lower = jnp.concatenate(rows, axis=0) * root
    out[0, 0] = jnp.dot(
        lower, values[...], precision=lax.Precision.HIGHEST, preferred_element_type=F32
    )


def call(kernel, shapes, specs, **extra):
    many = isinstance(shapes, (tuple, list))
    return pl.pallas_call(
        kernel,
        out_shape=shapes,
        in_specs=specs,
        out_specs=[VM] * len(shapes) if many else VM,
        compiler_params=pltpu.CompilerParams(vmem_limit_bytes=LIMIT),
        **extra,
    )


def shape(*dims, dtype=F32):
    return jax.ShapeDtypeStruct(dims, dtype)


def spread(value, combine, stages):
    for axis, bit in stages:
        value = combine(value, lax.ppermute(value, axis, xor_pairs(lax.axis_size(axis), bit)))
    return value


def per_device(basis, block_vals, block_cols, edge_rows, live_counts):
    vecs, cells = basis.shape[2:]
    blocks, slots, block = block_vals.shape[2:5]
    edges = edge_rows.shape[3]
    sizes = (lax.axis_size("gx"), lax.axis_size("gy"))
    field = shape(vecs, cells)
    sends = [shape(vecs, edges)] * 4

    place, *outgoing = call(edges_kernel, [shape(cells, 4 * edges, dtype=BF16)] + sends, [SM, VM, VM])(
        live_counts, edge_rows, basis
    )

    def exchange(parts):
        return [
            lax.ppermute(part, axis, swap_lists(lax.axis_size(axis), shift))
            for part, (axis, shift) in zip(parts, (("gx", 0), ("gx", 1), ("gy", 0), ("gy", 1)))
        ]

    arrived = exchange(outgoing)
    stored, inside, degree, peak = pl.pallas_call(
        functools.partial(first_product_kernel, sizes),
        grid=(blocks,),
        out_shape=[
            shape(blocks, 2 * block, slots * block, dtype=BF16),
            field,
            shape(8, cells),
            shape(8, LANES),
        ],
        in_specs=[
            SM,
            SM,
            pl.BlockSpec((1, 1, 1, slots, block, block), lambda m: (0, 0, m, 0, 0, 0)),
            VM,
            VM,
        ],
        out_specs=[VM] * 4,
        scratch_shapes=[pltpu.VMEM((vecs + 8, cells), F32)],
        compiler_params=pltpu.CompilerParams(vmem_limit_bytes=LIMIT),
    )(live_counts, block_cols, block_vals, basis, place)
    stages = [
        (axis, 1 << b) for axis, size in zip(("gx", "gy"), sizes) for b in range(size.bit_length() - 1)
    ]
    peak = spread(peak, jnp.maximum, stages)

    previous, current = basis, basis
    for number in range(DEGREE):
        last = number == DEGREE - 1
        following, *outgoing = call(
            functools.partial(combine_kernel, number),
            [field] + ([shape(vecs, vecs)] if last else sends),
            [SM] + [VM] * 10,
        )(live_counts, *arrived, inside, current, previous, degree, peak, place)
        previous, current = current, following
        if not last:
            arrived = exchange(outgoing)
            inside = call(product_kernel, field, [SM, VM, VM])(block_cols, current, stored)

    gram = spread(outgoing[0], jnp.add, stages[:-1])
    axis, bit = stages[-1]
    other = lax.ppermute(gram, axis, xor_pairs(lax.axis_size(axis), bit))
    root = math.sqrt(cells * sizes[0] * sizes[1])
    return call(functools.partial(encode_kernel, root), shape(1, 1, vecs, cells), [VM] * 3)(gram, other, current)


def solution(mesh):
    in_specs = (
        P("gx", "gy", None, None),
        P("gx", "gy", None, None, None, None),
        P("gx", "gy", None, None),
        P("gx", "gy", None, None),
        P("gx", "gy"),
    )
    out_specs = P("gx", "gy", None, None)
    return jax.shard_map(
        per_device, mesh=mesh, in_specs=in_specs, out_specs=out_specs, check_vma=False
    )
```

```python
import functools
import math

import jax
import jax.numpy as jnp
from jax import lax
from jax.experimental import pallas as pl
from jax.experimental.pallas import tpu as pltpu
from jax.sharding import PartitionSpec as P

DEGREE = 4
LOWER_FRACTION = 0.125
LANES = 128
CHUNK = 256
F32 = jnp.float32
BF16 = jnp.bfloat16
NT = (((1,), (1,)), ((), ()))
VM = pl.BlockSpec(memory_space=pltpu.VMEM)
SM = pl.BlockSpec(memory_space=pltpu.SMEM)
HBM = pl.BlockSpec(memory_space=pltpu.HBM)
LIMIT = 24 << 20
SIDES = (("gy", 1), ("gy", 0), ("gx", 1), ("gx", 0))


def split(x):
    hi = x.astype(BF16)
    return hi, (x - hi.astype(F32)).astype(BF16)


def stacked(x):
    return jnp.concatenate(split(x), axis=0)


def folded(x):
    half = x.shape[0] // 2
    return x[:half] + x[half:]


def dot(a, b):
    return jnp.dot(a, b, preferred_element_type=F32)


def swap_lists(size, shift):
    pairs = []
    for low in range(shift, size - 1, 2):
        pairs += [(low, low + 1), (low + 1, low)]
    return pairs


def xor_pairs(size, bit):
    return [(i, i ^ bit) for i in range(size)]


def live_lanes(count, start, width):
    return lax.broadcasted_iota(jnp.int32, (1, width), 1) + start < count


def left_rows(value):
    hi, lo = split(value)
    return [
        jnp.concatenate([hi, hi], axis=1),
        jnp.concatenate([lo, jnp.zeros_like(lo)], axis=1),
    ]


def first_kernel(sizes, cols, counts, lists_any, basis_any, weights_any, *refs):
    place, stored, begin, inside, degree, peak = refs[:6]
    outs = refs[6:10]
    lists, basis, weights, sems = refs[10:]
    blocks, slots = weights.shape[:2]
    vecs, cells = inside.shape
    edges = place.shape[1]
    width = edges // len(outs)
    loads = [
        pltpu.make_async_copy(lists_any.at[0, 0], lists, sems.at[blocks]),
        pltpu.make_async_copy(basis_any.at[0, 0], basis, sems.at[blocks + 1]),
    ]
    blocks_in = [
        pltpu.make_async_copy(weights_any.at[0, 0, m], weights.at[m], sems.at[m]) for m in range(blocks)
    ]
    for load in loads + blocks_in:
        load.start()
    count = counts[...]
    inside[...] = jnp.zeros_like(inside)
    degree[...] = jnp.zeros_like(degree)
    loads[0].wait()
    order, flags = [], []
    for axis, shift in SIDES:
        dim = ("gx", "gy").index(axis)
        me = lax.axis_index(axis)
        upward = me % 2 == shift
        low, high = lists[2 * dim : 2 * dim + 1], lists[2 * dim + 1 : 2 * dim + 2]
        order.append(jnp.where(upward, high, low))
        here = jnp.where(upward, me < sizes[dim] - 1, me > 0).astype(F32)
        flags.append(jnp.full((16, width), here, F32))
    targets = jnp.concatenate(order, axis=1)
    for start in range(0, cells, CHUNK):
        spot = lax.broadcasted_iota(jnp.int32, (CHUNK, edges), 0) + start
        place[start : start + CHUNK] = (spot == targets).astype(F32).astype(BF16)
    known = jnp.concatenate(flags, axis=1).astype(BF16)
    joined = lax.dot_general(known, place[...], NT, preferred_element_type=F32)[:8]
    loads[1].wait()
    begin[...] = jnp.where(live_lanes(count, 0, cells), basis[...], 0.0)
    picked = folded(dot(stacked(begin[...]), place[...]))
    for i, out in enumerate(outs):
        out[...] = picked[:, i * width : (i + 1) * width]
    for m in range(blocks):
        blocks_in[m].wait()
        for j in range(slots):
            hi, lo = split(weights[m, j])
            stored[m, 0:LANES, j * LANES : (j + 1) * LANES] = hi
            stored[m, LANES : 2 * LANES, j * LANES : (j + 1) * LANES] = lo
        part = slice(m * LANES, (m + 1) * LANES)
        live = live_lanes(count, m * LANES, LANES)
        ones = jnp.broadcast_to(live.astype(F32), (16, LANES)).astype(BF16)
        left = left_rows(begin[:, part])
        left.append(jnp.concatenate([ones, ones], axis=1))
        product = dot(jnp.concatenate(left, axis=0), stored[m])
        values = product[:vecs] + product[vecs : 2 * vecs]
        sums = product[2 * vecs : 2 * vecs + 8]
        for j in range(slots):
            spot = pl.ds(pl.multiple_of(cols[0, j, 0, m] * LANES, LANES), LANES)
            inside[:, spot] += values[:, j * LANES : (j + 1) * LANES]
            degree[:, spot] += sums[:, j * LANES : (j + 1) * LANES]
    value = jnp.where(live_lanes(count, 0, cells), degree[...] + joined, 0.0)
    degree[...] = value
    peak[...] = jnp.full(peak.shape, jnp.max(value), F32)


def product_kernel(cols, values, stored, inside):
    blocks, _, width = stored.shape
    inside[...] = jnp.zeros_like(inside)
    for m in range(blocks):
        left = left_rows(values[:, m * LANES : (m + 1) * LANES])
        product = folded(dot(jnp.concatenate(left, axis=0), stored[m]))
        for j in range(width // LANES):
            spot = pl.ds(pl.multiple_of(cols[0, j, 0, m] * LANES, LANES), LANES)
            inside[:, spot] += product[:, j * LANES : (j + 1) * LANES]


def combine_kernel(number, counts, r0, r1, r2, r3, inside, current, previous, degree, peak, place, following, *outs):
    cells, edges = place.shape
    count = counts[...]
    upper = 2.0 * peak[0:1, 0:1]
    lower = LOWER_FRACTION * upper
    half = (upper - lower) / 2.0
    centre = (upper + lower) / 2.0
    scale = (1.0 if number == 0 else 2.0) / half
    arrived = stacked(jnp.concatenate([r0[...], r1[...], r2[...], r3[...]], axis=1))
    for start in range(0, cells, CHUNK):
        part = slice(start, start + CHUNK)
        crossed = folded(
            lax.dot_general(arrived, place[part], NT, preferred_element_type=F32)
        )
        live = live_lanes(count, start, CHUNK)
        value = (degree[0:1, part] - centre) * current[:, part]
        value = scale * (value - jnp.where(live, inside[:, part] + crossed, 0.0))
        if number > 0:
            value = value - previous[:, part]
        following[:, part] = value
    if len(outs) == 1:
        whole = following[...]
        outs[0][...] = lax.dot_general(
            whole, whole, NT, precision=lax.Precision.HIGHEST, preferred_element_type=F32
        )
    else:
        picked = folded(dot(stacked(following[...]), place[...]))
        width = edges // len(outs)
        for i, out in enumerate(outs):
            out[...] = picked[:, i * width : (i + 1) * width]


def small_inverse(rows, start, size, width):
    near = [
        [jnp.broadcast_to(rows[i : i + 1, start + j : start + j + 1], (size, width)) for j in range(i + 1)]
        for i in range(size)
    ]
    far = [[None] * size for _ in range(size)]
    for k in range(size):
        pivot = near[k][k]
        inverse = 1.0 / pivot
        for i in range(k + 1, size):
            factor = near[i][k] * inverse
            for j in range(k + 1, i + 1):
                near[i][j] = near[i][j] - factor * near[j][k]
            for j in range(k):
                far[i][j] = far[i][j] - factor * far[k][j]
            far[i][k] = -factor
        root = lax.rsqrt(pivot)
        near[k] = root
    return [
        [far[i][j] * near[i] for j in range(i)] + [near[i]] for i in range(size)
    ]


def total(terms):
    terms = list(terms)
    while len(terms) > 1:
        terms = [a + b for a, b in zip(terms[::2], terms[1::2])] + terms[len(terms) & ~1 :]
    return terms[0]


def encode_kernel(root, first, second, values, out):
    gram = first[...] + second[...]
    vecs = gram.shape[0]
    size = 8
    lane = lax.broadcasted_iota(jnp.int32, (size, vecs), 1)
    sub = lax.broadcasted_iota(jnp.int32, (size, vecs), 0)
    rows = [gram[i * size : (i + 1) * size] for i in range(vecs // size)]
    for g in range(vecs // size):
        start = g * size
        inside = jnp.logical_and(lane >= start, lane < start + size)
        small = small_inverse(rows[g], start, size, vecs)
        unit = jnp.where(inside, (lane - start == sub).astype(F32), rows[g])
        spread_rows = [jnp.broadcast_to(unit[j : j + 1], (size, vecs)) for j in range(size)]
        half = [
            total(small[i][j] * spread_rows[j] for j in range(i + 1)) for i in range(size)
        ]
        whole = [
            total(small[i][j] * half[i] for i in range(j, size)) for j in range(size)
        ]
        for i in range(g + 1, vecs // size):
            kept = jnp.where(inside, 0.0, rows[i])
            rows[i] = kept - total(
                jnp.broadcast_to(rows[i][:, start + j : start + j + 1], (size, vecs)) * whole[j]
                for j in range(size)
            )
        done = half[0]
        for j in range(1, size):
            done = jnp.where(sub == j, half[j], done)
        rows[g] = jnp.where(lane < start + size, done, 0.0)
    lower = jnp.concatenate(rows, axis=0) * root
    out[0, 0] = jnp.dot(
        lower, values[...], precision=lax.Precision.HIGHEST, preferred_element_type=F32
    )


def call(kernel, shapes, specs, **extra):
    many = isinstance(shapes, (tuple, list))
    return pl.pallas_call(
        kernel,
        out_shape=shapes,
        in_specs=specs,
        out_specs=[VM] * len(shapes) if many else VM,
        compiler_params=pltpu.CompilerParams(vmem_limit_bytes=LIMIT),
        **extra,
    )


def shape(*dims, dtype=F32):
    return jax.ShapeDtypeStruct(dims, dtype)


def axis_bits(size):
    return size.bit_length() - 1


def spread(value, combine, stages):
    for axis, bit in stages:
        value = combine(value, lax.ppermute(value, axis, xor_pairs(lax.axis_size(axis), bit)))
    return value


def per_device(basis, block_vals, block_cols, edge_rows, live_counts):
    vecs, cells = basis.shape[2:]
    blocks, slots, block = block_vals.shape[2:5]
    edges = edge_rows.shape[3]
    sizes = (lax.axis_size("gx"), lax.axis_size("gy"))
    field = shape(vecs, cells)
    sends = [shape(vecs, edges)] * 4

    def exchange(parts):
        return [
            lax.ppermute(part, axis, swap_lists(lax.axis_size(axis), shift))
            for part, (axis, shift) in zip(parts, SIDES)
        ]

    cols = jnp.transpose(block_cols, (0, 3, 1, 2))
    place, stored, begin, inside, degree, peak, *outgoing = call(
        functools.partial(first_kernel, sizes),
        [
            shape(cells, 4 * edges, dtype=BF16),
            shape(blocks, 2 * block, slots * block, dtype=BF16),
            field,
            field,
            shape(8, cells),
            shape(8, LANES),
        ]
        + sends,
        [SM, VM] + [HBM] * 3,
        scratch_shapes=[
            pltpu.VMEM((4, edges), jnp.int32),
            pltpu.VMEM((vecs, cells), F32),
            pltpu.VMEM((blocks, slots, block, block), F32),
            pltpu.SemaphoreType.DMA((blocks + 2,)),
        ],
    )(cols, live_counts, *(pltpu.with_memory_space_constraint(x, pltpu.HBM) for x in (edge_rows, basis, block_vals)))
    stages = [
        (axis, 1 << b) for axis, size in zip(("gx", "gy"), sizes) for b in range(axis_bits(size))
    ]
    arrived, queue = [], list(zip(outgoing, SIDES))
    for axis, bit in (stages[0], *stages[axis_bits(sizes[0]) :], *stages[1 : axis_bits(sizes[0])]):
        if queue:
            part, (side, shift) = queue.pop(0)
            peak, part = lax.optimization_barrier((peak, part))
            arrived.append(lax.ppermute(part, side, swap_lists(lax.axis_size(side), shift)))
        peak = jnp.maximum(peak, lax.ppermute(peak, axis, xor_pairs(lax.axis_size(axis), bit)))

    previous, current = begin, begin
    for number in range(DEGREE):
        last = number == DEGREE - 1
        following, *outgoing = call(
            functools.partial(combine_kernel, number),
            [field] + ([shape(vecs, vecs)] if last else sends),
            [VM] * 11,
        )(live_counts, *arrived, inside, current, previous, degree, peak, place)
        previous, current = current, following
        if not last:
            arrived = exchange(outgoing)
            inside = call(product_kernel, field, [SM, VM, VM])(cols, current, stored)

    gram = spread(outgoing[0], jnp.add, stages[:-1])
    axis, bit = stages[-1]
    other = lax.ppermute(gram, axis, xor_pairs(lax.axis_size(axis), bit))
    root = math.sqrt(cells * sizes[0] * sizes[1])
    return call(functools.partial(encode_kernel, root), shape(1, 1, vecs, cells), [VM] * 3)(gram, other, current)


def solution(mesh):
    in_specs = (
        P("gx", "gy", None, None),
        P("gx", "gy", None, None, None, None),
        P("gx", "gy", None, None),
        P("gx", "gy", None, None),
        P("gx", "gy"),
    )
    out_specs = P("gx", "gy", None, None)
    return jax.shard_map(
        per_device, mesh=mesh, in_specs=in_specs, out_specs=out_specs, check_vma=False
    )
```

```python
import functools
import math

import jax
import jax.numpy as jnp
from jax import lax
from jax.experimental import pallas as pl
from jax.experimental.pallas import tpu as pltpu
from jax.sharding import PartitionSpec as P

LOWER_FRACTION = 0.125
LANES = 128
CHUNK = 256
F32 = jnp.float32
BF16 = jnp.bfloat16
EXACT = lax.Precision.HIGHEST
NT = (((1,), (1,)), ((), ()))
VM = pl.BlockSpec(memory_space=pltpu.VMEM)
SM = pl.BlockSpec(memory_space=pltpu.SMEM)
HBM = pl.BlockSpec(memory_space=pltpu.HBM)
LIMIT = 24 << 20
SIDES = (("gx", 1), ("gy", 1), ("gy", 0), ("gx", 0))


def split(x):
    hi = x.astype(BF16)
    return hi, (x - hi.astype(F32)).astype(BF16)


def stacked(x):
    return jnp.concatenate(split(x), axis=0)


def folded(x):
    half = x.shape[0] // 2
    return x[:half] + x[half:]


def dot(a, b):
    return jnp.dot(a, b, preferred_element_type=F32)


def dot_nt(a, b, **extra):
    return lax.dot_general(a, b, NT, preferred_element_type=F32, **extra)


def near_pairs(size):
    return [(i, i ^ 1) for i in range(size)]


def far_pairs(size):
    return [(i, (i + 1 if i % 2 else i - 1) % size) for i in range(size)]


def turn_pairs(size):
    up = [(i, i + 2 if i + 2 < size else i + 1) for i in range(0, size, 2)]
    down = [(i, i - 2 if i > 1 else 0) for i in range(1, size, 2)]
    return up + down


def xor_pairs(size, bit):
    return [(i, i ^ bit) for i in range(size)]


def live_lanes(count, start, width):
    return lax.broadcasted_iota(jnp.int32, (1, width), 1) + start < count


def left_rows(value):
    hi, lo = split(value)
    return jnp.concatenate(
        [
            jnp.concatenate([hi, hi], axis=1),
            jnp.concatenate([lo, jnp.zeros_like(lo)], axis=1),
        ],
        axis=0,
    )


def scalars(peak):
    upper = 2.0 * peak[0:1, 0:1]
    lower = LOWER_FRACTION * upper
    return (upper + lower) / 2.0, (upper - lower) / 2.0


def first_kernel(sizes, cols, counts, lists_any, basis_any, weights_any, *refs):
    place, stored, begin, degree, peak, marks = refs[:6]
    outs = refs[6:10]
    lists, basis, weights, sems = refs[10:]
    blocks, slots = weights.shape[:2]
    cells, edges = place.shape
    width = edges // len(outs)
    loads = [
        pltpu.make_async_copy(lists_any.at[0, 0], lists, sems.at[blocks]),
        pltpu.make_async_copy(basis_any.at[0, 0], basis, sems.at[blocks + 1]),
    ]
    blocks_in = [
        pltpu.make_async_copy(weights_any.at[0, 0, m], weights.at[m], sems.at[m]) for m in range(blocks)
    ]
    for load in loads + blocks_in:
        load.start()
    count = counts[...]
    degree[...] = jnp.zeros_like(degree)
    loads[0].wait()
    order = []
    for axis, shift in SIDES:
        dim = ("gx", "gy").index(axis)
        me = lax.axis_index(axis)
        upward = me % 2 == shift
        low, high = lists[2 * dim : 2 * dim + 1], lists[2 * dim + 1 : 2 * dim + 2]
        low, high = jnp.where(me > 0, low, -1), jnp.where(me < sizes[dim] - 1, high, -1)
        order.append(jnp.where(upward, high, low))
    targets = jnp.concatenate(order, axis=1)
    marks[...] = jnp.broadcast_to(targets, marks.shape)
    for start in range(0, cells, CHUNK):
        spot = lax.broadcasted_iota(jnp.int32, (CHUNK, edges), 0) + start
        place[start : start + CHUNK] = (spot == targets).astype(F32).astype(BF16)
    loads[1].wait()
    begin[...] = jnp.where(live_lanes(count, 0, cells), basis[...], 0.0)
    picked = folded(dot(stacked(begin[...]), place[...]))
    for i, out in enumerate(outs):
        out[...] = picked[:, i * width : (i + 1) * width]
    joined = dot_nt(jnp.ones((16, edges), BF16), place[...])[:8]
    for m in range(blocks):
        blocks_in[m].wait()
        for j in range(slots):
            hi, lo = split(weights[m, j])
            stored[m, 0:LANES, j * LANES : (j + 1) * LANES] = hi
            stored[m, LANES : 2 * LANES, j * LANES : (j + 1) * LANES] = lo
        live = live_lanes(count, m * LANES, LANES)
        ones = jnp.broadcast_to(live.astype(F32), (16, LANES)).astype(BF16)
        sums = dot(jnp.concatenate([ones, ones], axis=1), stored[m])[:8]
        for j in range(slots):
            spot = pl.ds(pl.multiple_of(cols[0, j, 0, m] * LANES, LANES), LANES)
            degree[:, spot] += sums[:, j * LANES : (j + 1) * LANES]
    value = jnp.where(live_lanes(count, 0, cells), degree[...] + joined, 0.0)
    degree[...] = value
    peak[...] = jnp.full(peak.shape, jnp.max(value), F32)


def multiply(cols, values, stored, inside):
    blocks, _, width = stored.shape
    inside[...] = jnp.zeros_like(inside)
    for m in range(blocks):
        product = folded(dot(left_rows(values[:, m * LANES : (m + 1) * LANES]), stored[m]))
        for j in range(width // LANES):
            spot = pl.ds(pl.multiple_of(cols[0, j, 0, m] * LANES, LANES), LANES)
            inside[:, spot] += product[:, j * LANES : (j + 1) * LANES]


def gather(values, place):
    return folded(dot(stacked(values), place[...]))


def joined_up(parts):
    return jnp.concatenate([part[...] for part in parts], axis=1)


def chunks(cells):
    return [slice(start, start + CHUNK) for start in range(0, cells, CHUNK)]


def open_kernel(cols, counts, begin, stored, degree, place, marks, local, edge_local, same, inside):
    cells, edges = place.shape
    targets = marks[0:1]
    for start in range(0, edges, LANES):
        across = jnp.broadcast_to(targets[:, start : start + LANES], (LANES, LANES))
        down = across.astype(F32).T.astype(jnp.int32)
        down = jnp.where(down < 0, -2, down)
        for other in range(0, edges, LANES):
            equal = down == targets[:, other : other + LANES]
            same[start : start + LANES, other : other + LANES] = equal.astype(F32).astype(BF16)
    multiply(cols, begin, stored, inside)
    for part in chunks(cells):
        live = live_lanes(counts[...], part.start, CHUNK)
        local[:, part] = degree[0:1, part] * begin[:, part] - jnp.where(live, inside[:, part], 0.0)
    edge_local[...] = gather(local[...], place)


def edges_kernel(number, r0, r1, r2, r3, edge_local, same, own, peak, before, *outs):
    crossed = folded(dot(stacked(joined_up((r0, r1, r2, r3))), same[...]))
    if number == 0:
        value = edge_local[...] - crossed
    elif number == 1:
        centre, half = scalars(peak)
        top = own[0:1, 0:1]
        first, second = joined_up(before[:4]), joined_up(before[4:])
        value = second_field(centre, half, top, edge_local[...] - crossed / top, second, first)[1]
    else:
        _, half = scalars(peak)
        value = edge_local[...] - (2.0 / half) * crossed
    width = value.shape[1] // len(outs)
    for i, out in enumerate(outs):
        out[...] = value[:, i * width : (i + 1) * width]


def second_field(centre, half, top, twice, once, begin):
    ratio = centre / half
    shrunk = once / half
    first = shrunk - ratio * begin
    second = (2.0 / half) * (top / half) * twice - 2.0 * ratio * (shrunk + first) - begin
    return first, second


def field_kernel(number, cols, counts, r0, r1, r2, r3, local, stored, degree, place, own, peak, begin, once, *refs):
    field, later, edge_local = refs[:3]
    inside = refs[-1]
    cells = place.shape[0]
    top = own[0:1, 0:1]
    centre, half = scalars(peak)
    arrived = stacked(joined_up((r0, r1, r2, r3)))
    for part in chunks(cells):
        crossed = folded(dot_nt(arrived, place[part]))
        if number == 0:
            field[:, part] = (local[:, part] - crossed) / top
        elif number == 1:
            first, field[:, part] = second_field(
                centre, half, top, local[:, part] - crossed / top, once[:, part] * top, begin[:, part]
            )
            later[:, part] = first
        else:
            field[:, part] = local[:, part] - (2.0 / half) * crossed
            later[:, part] = begin[:, part]
    multiply(cols, field, stored, inside)
    for part in chunks(cells):
        live = live_lanes(counts[...], part.start, CHUNK)
        kept = jnp.where(live, inside[:, part], 0.0)
        if number == 0:
            later[:, part] = degree[0:1, part] * field[:, part] - kept
        else:
            value = (degree[0:1, part] - centre) * field[:, part] - kept
            later[:, part] = (2.0 / half) * value - later[:, part]
    edge_local[...] = gather(later[...], place)
    if number == 2:
        refs[3][...] = dot_nt(later[...], later[...], precision=EXACT)


def gram_kernel(r0, r1, r2, r3, edge_local, same, peak, base, gram):
    _, half = scalars(peak)
    scale = 2.0 / half
    arrived = joined_up((r0, r1, r2, r3))
    crossed = folded(dot(stacked(arrived), same[...]))
    mixed = dot_nt(scale * (edge_local[...] - (0.5 * scale) * crossed), arrived, precision=EXACT)
    gram[...] = base[...] - mixed - mixed.T


def last_kernel(r0, r1, r2, r3, local, place, peak, field):
    _, half = scalars(peak)
    arrived = stacked(joined_up((r0, r1, r2, r3)))
    for part in chunks(place.shape[0]):
        field[:, part] = local[:, part] - (2.0 / half) * folded(dot_nt(arrived, place[part]))


def small_inverse(rows, start, size, width):
    near = [
        [jnp.broadcast_to(rows[i : i + 1, start + j : start + j + 1], (size, width)) for j in range(i + 1)]
        for i in range(size)
    ]
    far = [[None] * size for _ in range(size)]
    for k in range(size):
        pivot = near[k][k]
        inverse = 1.0 / pivot
        for i in range(k + 1, size):
            factor = near[i][k] * inverse
            for j in range(k + 1, i + 1):
                near[i][j] = near[i][j] - factor * near[j][k]
            for j in range(k):
                far[i][j] = far[i][j] - factor * far[k][j]
            far[i][k] = -factor
        root = lax.rsqrt(pivot)
        near[k] = root
    return [
        [far[i][j] * near[i] for j in range(i)] + [near[i]] for i in range(size)
    ]


def total(terms):
    terms = list(terms)
    while len(terms) > 1:
        terms = [a + b for a, b in zip(terms[::2], terms[1::2])] + terms[len(terms) & ~1 :]
    return terms[0]


def encode_kernel(root, first, second, values, out):
    gram = first[...] + second[...]
    vecs = gram.shape[0]
    size = 8
    lane = lax.broadcasted_iota(jnp.int32, (size, vecs), 1)
    sub = lax.broadcasted_iota(jnp.int32, (size, vecs), 0)
    rows = [gram[i * size : (i + 1) * size] for i in range(vecs // size)]
    for g in range(vecs // size):
        start = g * size
        inside = jnp.logical_and(lane >= start, lane < start + size)
        small = small_inverse(rows[g], start, size, vecs)
        unit = jnp.where(inside, (lane - start == sub).astype(F32), rows[g])
        spread_rows = [jnp.broadcast_to(unit[j : j + 1], (size, vecs)) for j in range(size)]
        half = [
            total(small[i][j] * spread_rows[j] for j in range(i + 1)) for i in range(size)
        ]
        whole = [
            total(small[i][j] * half[i] for i in range(j, size)) for j in range(size)
        ]
        for i in range(g + 1, vecs // size):
            kept = jnp.where(inside, 0.0, rows[i])
            rows[i] = kept - total(
                jnp.broadcast_to(rows[i][:, start + j : start + j + 1], (size, vecs)) * whole[j]
                for j in range(size)
            )
        done = half[0]
        for j in range(1, size):
            done = jnp.where(sub == j, half[j], done)
        rows[g] = jnp.where(lane < start + size, done, 0.0)
    lower = jnp.concatenate(rows, axis=0) * root
    out[0, 0] = jnp.dot(
        lower, values[...], precision=EXACT, preferred_element_type=F32
    )


def call(kernel, shapes, specs, **extra):
    many = isinstance(shapes, (tuple, list))
    return pl.pallas_call(
        kernel,
        out_shape=shapes,
        in_specs=specs,
        out_specs=[VM] * len(shapes) if many else VM,
        compiler_params=pltpu.CompilerParams(vmem_limit_bytes=LIMIT),
        **extra,
    )


def shape(*dims, dtype=F32):
    return jax.ShapeDtypeStruct(dims, dtype)


def spread(value, combine, stages):
    for axis, bit in stages:
        value = combine(value, lax.ppermute(value, axis, xor_pairs(lax.axis_size(axis), bit)))
    return value


def per_device(basis, block_vals, block_cols, edge_rows, live_counts):
    vecs, cells = basis.shape[2:]
    blocks, slots, block = block_vals.shape[2:5]
    edges = edge_rows.shape[3]
    sizes = (lax.axis_size("gx"), lax.axis_size("gy"))
    field = shape(vecs, cells)
    sends = [shape(vecs, edges)] * 4
    edge_field = shape(vecs, 4 * edges)
    scratch = [pltpu.VMEM((vecs, cells), F32)]

    def exchange(parts):
        x_far, y_far, y_near, x_near = parts
        x_far = lax.ppermute(x_far, "gx", near_pairs(sizes[0]))
        y_far = lax.ppermute(y_far, "gy", far_pairs(sizes[1]))
        y_near = lax.ppermute(y_near, "gy", near_pairs(sizes[1]))
        x_far = lax.ppermute(x_far, "gx", turn_pairs(sizes[0]))
        x_near = lax.ppermute(x_near, "gx", near_pairs(sizes[0]))
        return [x_far, y_far, y_near, x_near]

    cols = jnp.transpose(block_cols, (0, 3, 1, 2))
    place, stored, begin, degree, own, marks, *outgoing = call(
        functools.partial(first_kernel, sizes),
        [
            shape(cells, 4 * edges, dtype=BF16),
            shape(blocks, 2 * block, slots * block, dtype=BF16),
            field,
            shape(8, cells),
            shape(8, LANES),
            shape(8, 4 * edges, dtype=jnp.int32),
        ]
        + sends,
        [SM, VM] + [HBM] * 3,
        scratch_shapes=[
            pltpu.VMEM((4, edges), jnp.int32),
            pltpu.VMEM((vecs, cells), F32),
            pltpu.VMEM((blocks, slots, block, block), F32),
            pltpu.SemaphoreType.DMA((blocks + 2,)),
        ],
    )(
        cols,
        live_counts,
        *(pltpu.with_memory_space_constraint(x, pltpu.HBM) for x in (edge_rows, basis, block_vals)),
    )
    stages = [
        (axis, 1 << b) for axis, size in zip(("gx", "gy"), sizes) for b in range(size.bit_length() - 1)
    ]
    arrived = exchange(outgoing)
    peak = spread(own, jnp.maximum, stages)
    local, edge_local, same = call(
        open_kernel,
        [field, edge_field, shape(4 * edges, 4 * edges, dtype=BF16)],
        [SM] + [VM] * 6,
        scratch_shapes=scratch,
    )(cols, live_counts, begin, stored, degree, place, marks)

    history, earlier = [outgoing], [begin, begin]
    for number in range(3):
        bound = peak if number else own
        before = [x for parts in history for x in parts] if number == 1 else []
        outgoing = call(
            lambda *refs, number=number, count=len(before): edges_kernel(
                number, *refs[:8], refs[8 : 8 + count], *refs[8 + count :]
            ),
            sends,
            [VM] * (8 + len(before)),
        )(*arrived, edge_local, same, own, bound, *before)
        history.append(outgoing)
        coming = exchange(outgoing)
        now, local, edge_local, *base = call(
            functools.partial(field_kernel, number),
            [field, field, edge_field] + [shape(vecs, vecs)] * (number == 2),
            [SM] + [VM] * 13,
            scratch_shapes=scratch,
        )(cols, live_counts, *arrived, local, stored, degree, place, own, bound, *earlier)
        earlier = [begin, now] if number == 0 else [now, now]
        arrived = coming

    gram = call(gram_kernel, shape(vecs, vecs), [VM] * 8)(*arrived, edge_local, same, peak, *base)
    gram = spread(gram, jnp.add, stages[:-1])
    axis, bit = stages[-1]
    other = lax.ppermute(gram, axis, xor_pairs(lax.axis_size(axis), bit))
    now = call(last_kernel, field, [VM] * 7)(*arrived, local, place, peak)
    root = math.sqrt(cells * sizes[0] * sizes[1])
    return call(functools.partial(encode_kernel, root), shape(1, 1, vecs, cells), [VM] * 3)(gram, other, now)


def solution(mesh):
    in_specs = (
        P("gx", "gy", None, None),
        P("gx", "gy", None, None, None, None),
        P("gx", "gy", None, None),
        P("gx", "gy", None, None),
        P("gx", "gy"),
    )
    out_specs = P("gx", "gy", None, None)
    return jax.shard_map(
        per_device, mesh=mesh, in_specs=in_specs, out_specs=out_specs, check_vma=False
    )
```

```python
import functools
import math

import jax
import jax.numpy as jnp
from jax import lax
from jax.experimental import pallas as pl
from jax.experimental.pallas import tpu as pltpu
from jax.sharding import PartitionSpec as P


LOWER_FRACTION = 0.125
LANES = 128
CHUNK = 256
F32 = jnp.float32
BF16 = jnp.bfloat16
NT = (((1,), (1,)), ((), ()))
VM = pl.BlockSpec(memory_space=pltpu.VMEM)
SM = pl.BlockSpec(memory_space=pltpu.SMEM)
HBM = pl.BlockSpec(memory_space=pltpu.HBM)
LIMIT = 24 << 20
SIDES = (("gx", 1), ("gy", 1), ("gy", 0), ("gx", 0))


def split(x):
    hi = x.astype(BF16)
    return hi, (x - hi.astype(F32)).astype(BF16)


def stacked(x):
    return jnp.concatenate(split(x), axis=0)


def folded(x):
    half = x.shape[0] // 2
    return x[:half] + x[half:]


def dot(a, b):
    return jnp.dot(a, b, preferred_element_type=F32)


def dot_nt(a, b):
    return lax.dot_general(a, b, NT, preferred_element_type=F32)


def product_nt(a, b):
    left, right = stacked(a), stacked(b)
    product = folded(dot_nt(left, right))
    half = product.shape[1] // 2
    return product[:, :half] + product[:, half:]


def near_pairs(size):
    return [(i, i ^ 1) for i in range(size)]


def far_pairs(size):
    return [(i, (i + 1 if i % 2 else i - 1) % size) for i in range(size)]


def turn_pairs(size):
    up = [(i, i + 2 if i + 2 < size else i + 1) for i in range(0, size, 2)]
    down = [(i, i - 2 if i > 1 else 0) for i in range(1, size, 2)]
    return up + down


def xor_pairs(size, bit):
    return [(i, i ^ bit) for i in range(size)]


def live_lanes(count, start, width):
    return lax.broadcasted_iota(jnp.int32, (1, width), 1) + start < count


def left_rows(value):
    hi, lo = split(value)
    return jnp.concatenate(
        [
            jnp.concatenate([hi, hi], axis=1),
            jnp.concatenate([lo, jnp.zeros_like(lo)], axis=1),
        ],
        axis=0,
    )


def scalars(peak):
    upper = 2.0 * peak[0:1, 0:1]
    lower = LOWER_FRACTION * upper
    return (upper + lower) / 2.0, (upper - lower) / 2.0


def first_kernel(sizes, cols, counts, lists_any, basis_any, weights_any, *refs):
    place, stored, begin, degree, peak, marks = refs[:6]
    outs = refs[6:10]
    lists, basis, weights, sems = refs[10:]
    blocks, slots = weights.shape[:2]
    cells, edges = place.shape
    width = edges // len(outs)
    loads = [
        pltpu.make_async_copy(lists_any.at[0, 0], lists, sems.at[blocks]),
        pltpu.make_async_copy(basis_any.at[0, 0], basis, sems.at[blocks + 1]),
    ]
    blocks_in = [
        pltpu.make_async_copy(weights_any.at[0, 0, m], weights.at[m], sems.at[m]) for m in range(blocks)
    ]
    for load in loads + blocks_in:
        load.start()
    count = counts[...]
    degree[...] = jnp.zeros_like(degree)
    loads[0].wait()
    order = []
    for axis, shift in SIDES:
        dim = ("gx", "gy").index(axis)
        me = lax.axis_index(axis)
        upward = me % 2 == shift
        low, high = lists[2 * dim : 2 * dim + 1], lists[2 * dim + 1 : 2 * dim + 2]
        low, high = jnp.where(me > 0, low, -1), jnp.where(me < sizes[dim] - 1, high, -1)
        order.append(jnp.where(upward, high, low))
    targets = jnp.concatenate(order, axis=1)
    marks[...] = jnp.broadcast_to(targets, marks.shape)
    for start in range(0, cells, CHUNK):
        spot = lax.broadcasted_iota(jnp.int32, (CHUNK, edges), 0) + start
        place[start : start + CHUNK] = (spot == targets).astype(F32).astype(BF16)
    loads[1].wait()
    begin[...] = jnp.where(live_lanes(count, 0, cells), basis[...], 0.0)
    picked = folded(dot(stacked(begin[...]), place[...]))
    for i, out in enumerate(outs):
        out[...] = picked[:, i * width : (i + 1) * width]
    joined = dot_nt(jnp.ones((16, edges), BF16), place[...])[:8]
    for m in range(blocks):
        blocks_in[m].wait()
        for j in range(slots):
            hi, lo = split(weights[m, j])
            stored[m, 0:LANES, j * LANES : (j + 1) * LANES] = hi
            stored[m, LANES : 2 * LANES, j * LANES : (j + 1) * LANES] = lo
        live = live_lanes(count, m * LANES, LANES)
        ones = jnp.broadcast_to(live.astype(F32), (16, LANES)).astype(BF16)
        sums = dot(jnp.concatenate([ones, ones], axis=1), stored[m])[:8]
        for j in range(slots):
            spot = pl.ds(pl.multiple_of(cols[0, j, 0, m] * LANES, LANES), LANES)
            degree[:, spot] += sums[:, j * LANES : (j + 1) * LANES]
    value = jnp.where(live_lanes(count, 0, cells), degree[...] + joined, 0.0)
    degree[...] = value
    peak[...] = jnp.full(peak.shape, jnp.max(value), F32)


def multiply(cols, values, stored, inside):
    blocks, _, width = stored.shape
    inside[...] = jnp.zeros_like(inside)
    for m in range(blocks):
        product = folded(dot(left_rows(values[:, m * LANES : (m + 1) * LANES]), stored[m]))
        for j in range(width // LANES):
            spot = pl.ds(pl.multiple_of(cols[0, j, 0, m] * LANES, LANES), LANES)
            inside[:, spot] += product[:, j * LANES : (j + 1) * LANES]


def gather(values, place):
    return folded(dot(stacked(values), place[...]))


def joined_up(parts):
    return jnp.concatenate([part[...] for part in parts], axis=1)


def chunks(cells):
    return [slice(start, start + CHUNK) for start in range(0, cells, CHUNK)]


def open_kernel(cols, counts, begin, stored, degree, place, marks, local, edge_local, same, inside):
    cells, edges = place.shape
    targets = marks[0:1]
    for start in range(0, edges, LANES):
        across = jnp.broadcast_to(targets[:, start : start + LANES], (LANES, LANES))
        down = across.astype(F32).T.astype(jnp.int32)
        down = jnp.where(down < 0, -2, down)
        for other in range(0, edges, LANES):
            equal = down == targets[:, other : other + LANES]
            same[start : start + LANES, other : other + LANES] = equal.astype(F32).astype(BF16)
    multiply(cols, begin, stored, inside)
    for part in chunks(cells):
        live = live_lanes(counts[...], part.start, CHUNK)
        local[:, part] = degree[0:1, part] * begin[:, part] - jnp.where(live, inside[:, part], 0.0)
    edge_local[...] = gather(local[...], place)


def edges_kernel(number, r0, r1, r2, r3, edge_local, same, own, peak, before, *outs):
    crossed = folded(dot(stacked(joined_up((r0, r1, r2, r3))), same[...]))
    if number == 0:
        value = edge_local[...] - crossed
    elif number == 1:
        centre, half = scalars(peak)
        top = own[0:1, 0:1]
        first, second = joined_up(before[:4]), joined_up(before[4:])
        value = second_field(centre, half, top, edge_local[...] - crossed / top, second, first)[1]
    else:
        _, half = scalars(peak)
        value = edge_local[...] - (2.0 / half) * crossed
    width = value.shape[1] // len(outs)
    for i, out in enumerate(outs):
        out[...] = value[:, i * width : (i + 1) * width]


def second_field(centre, half, top, twice, once, begin):
    ratio = centre / half
    shrunk = once / half
    first = shrunk - ratio * begin
    second = (2.0 / half) * (top / half) * twice - 2.0 * ratio * (shrunk + first) - begin
    return first, second


def field_kernel(number, cols, counts, r0, r1, r2, r3, local, stored, degree, place, own, peak, begin, once, *refs):
    field, later, edge_local = refs[:3]
    inside = refs[-1]
    cells = place.shape[0]
    top = own[0:1, 0:1]
    centre, half = scalars(peak)
    arrived = stacked(joined_up((r0, r1, r2, r3)))
    for part in chunks(cells):
        crossed = folded(dot_nt(arrived, place[part]))
        if number == 0:
            field[:, part] = (local[:, part] - crossed) / top
        elif number == 1:
            first, field[:, part] = second_field(
                centre, half, top, local[:, part] - crossed / top, once[:, part] * top, begin[:, part]
            )
            later[:, part] = first
        else:
            field[:, part] = local[:, part] - (2.0 / half) * crossed
            later[:, part] = begin[:, part]
    multiply(cols, field, stored, inside)
    for part in chunks(cells):
        live = live_lanes(counts[...], part.start, CHUNK)
        kept = jnp.where(live, inside[:, part], 0.0)
        if number == 0:
            later[:, part] = degree[0:1, part] * field[:, part] - kept
        else:
            value = (degree[0:1, part] - centre) * field[:, part] - kept
            later[:, part] = (2.0 / half) * value - later[:, part]
    edge_local[...] = gather(later[...], place)
    if number == 2:
        refs[3][...] = product_nt(later[...], later[...])


def gram_kernel(r0, r1, r2, r3, edge_local, same, peak, base, gram):
    _, half = scalars(peak)
    scale = 2.0 / half
    arrived = joined_up((r0, r1, r2, r3))
    crossed = folded(dot(stacked(arrived), same[...]))
    mixed = product_nt(scale * (edge_local[...] - (0.5 * scale) * crossed), arrived)
    gram[...] = base[...] - mixed - mixed.T


def last_kernel(r0, r1, r2, r3, local, place, peak, terms):
    _, half = scalars(peak)
    arrived = stacked(joined_up((r0, r1, r2, r3)))
    for part in chunks(place.shape[0]):
        hi, lo = split(local[:, part] - (2.0 / half) * folded(dot_nt(arrived, place[part])))
        terms[:, part] = jnp.concatenate([hi, lo, hi], axis=0)


def small_inverse(rows, start, size, width):
    near = [
        [jnp.broadcast_to(rows[i : i + 1, start + j : start + j + 1], (size, width)) for j in range(i + 1)]
        for i in range(size)
    ]
    far = [[None] * size for _ in range(size)]
    for k in range(size):
        pivot = near[k][k]
        inverse = 1.0 / pivot
        for i in range(k + 1, size):
            factor = near[i][k] * inverse
            for j in range(k + 1, i + 1):
                near[i][j] = near[i][j] - factor * near[j][k]
            for j in range(k):
                far[i][j] = far[i][j] - factor * far[k][j]
            far[i][k] = -factor
        root = lax.rsqrt(pivot)
        near[k] = root
    return [
        [far[i][j] * near[i] for j in range(i)] + [near[i]] for i in range(size)
    ]


def total(terms):
    terms = list(terms)
    while len(terms) > 1:
        terms = [a + b for a, b in zip(terms[::2], terms[1::2])] + terms[len(terms) & ~1 :]
    return terms[0]


def encode_kernel(root, first, second, values, out):
    gram = first[...] + second[...]
    vecs = gram.shape[0]
    size = 8
    lane = lax.broadcasted_iota(jnp.int32, (size, vecs), 1)
    sub = lax.broadcasted_iota(jnp.int32, (size, vecs), 0)
    rows = [gram[i * size : (i + 1) * size] for i in range(vecs // size)]
    for g in range(vecs // size):
        start = g * size
        inside = jnp.logical_and(lane >= start, lane < start + size)
        small = small_inverse(rows[g], start, size, vecs)
        unit = jnp.where(inside, (lane - start == sub).astype(F32), rows[g])
        spread_rows = [jnp.broadcast_to(unit[j : j + 1], (size, vecs)) for j in range(size)]
        half = [
            total(small[i][j] * spread_rows[j] for j in range(i + 1)) for i in range(size)
        ]
        whole = [
            total(small[i][j] * half[i] for i in range(j, size)) for j in range(size)
        ]
        for i in range(g + 1, vecs // size):
            kept = jnp.where(inside, 0.0, rows[i])
            rows[i] = kept - total(
                jnp.broadcast_to(rows[i][:, start + j : start + j + 1], (size, vecs)) * whole[j]
                for j in range(size)
            )
        done = half[0]
        for j in range(1, size):
            done = jnp.where(sub == j, half[j], done)
        rows[g] = jnp.where(lane < start + size, done, 0.0)
    hi, lo = split(jnp.concatenate(rows, axis=0) * root)
    out[0, 0] = dot(jnp.concatenate([hi, hi, lo], axis=1), values[...])


def call(kernel, shapes, specs, **extra):
    many = isinstance(shapes, (tuple, list))
    return pl.pallas_call(
        kernel,
        out_shape=shapes,
        in_specs=specs,
        out_specs=[VM] * len(shapes) if many else VM,
        compiler_params=pltpu.CompilerParams(vmem_limit_bytes=LIMIT),
        **extra,
    )


def shape(*dims, dtype=F32):
    return jax.ShapeDtypeStruct(dims, dtype)


def spread(value, combine, stages):
    for axis, bit in stages:
        pairs = xor_pairs(lax.axis_size(axis), bit)
        value = combine(value, lax.ppermute(value, axis, pairs))
    return value


def per_device(basis, block_vals, block_cols, edge_rows, live_counts):
    vecs, cells = basis.shape[2:]
    blocks, slots, block = block_vals.shape[2:5]
    edges = edge_rows.shape[3]
    sizes = (lax.axis_size("gx"), lax.axis_size("gy"))
    field = shape(vecs, cells)
    sends = [shape(vecs, edges)] * 4
    edge_field = shape(vecs, 4 * edges)
    scratch = [pltpu.VMEM((vecs, cells), F32)]

    def exchange(parts):
        x_far, y_far, y_near, x_near = parts
        x_far = lax.ppermute(x_far, "gx", near_pairs(sizes[0]))
        y_far = lax.ppermute(y_far, "gy", far_pairs(sizes[1]))
        y_near = lax.ppermute(y_near, "gy", near_pairs(sizes[1]))
        x_far = lax.ppermute(x_far, "gx", turn_pairs(sizes[0]))
        x_near = lax.ppermute(x_near, "gx", near_pairs(sizes[0]))
        return [x_far, y_far, y_near, x_near]

    cols = jnp.transpose(block_cols, (0, 3, 1, 2))
    place, stored, begin, degree, own, marks, *outgoing = call(
        functools.partial(first_kernel, sizes),
        [
            shape(cells, 4 * edges, dtype=BF16),
            shape(blocks, 2 * block, slots * block, dtype=BF16),
            field,
            shape(8, cells),
            shape(8, LANES),
            shape(8, 4 * edges, dtype=jnp.int32),
        ]
        + sends,
        [SM, VM] + [HBM] * 3,
        scratch_shapes=[
            pltpu.VMEM((4, edges), jnp.int32),
            pltpu.VMEM((vecs, cells), F32),
            pltpu.VMEM((blocks, slots, block, block), F32),
            pltpu.SemaphoreType.DMA((blocks + 2,)),
        ],
    )(
        cols,
        live_counts,
        *(pltpu.with_memory_space_constraint(x, pltpu.HBM) for x in (edge_rows, basis, block_vals)),
    )
    stages = [
        (axis, 1 << b) for axis, size in zip(("gx", "gy"), sizes) for b in range(size.bit_length() - 1)
    ]
    arrived = exchange(outgoing)
    peak = spread(own, jnp.maximum, stages)
    local, edge_local, same = call(
        open_kernel,
        [field, edge_field, shape(4 * edges, 4 * edges, dtype=BF16)],
        [SM] + [VM] * 6,
        scratch_shapes=scratch,
    )(cols, live_counts, begin, stored, degree, place, marks)

    history, earlier = [outgoing], [begin, begin]
    for number in range(3):
        bound = peak if number else own
        before = [x for parts in history for x in parts] if number == 1 else []
        outgoing = call(
            lambda *refs, number=number, count=len(before): edges_kernel(
                number, *refs[:8], refs[8 : 8 + count], *refs[8 + count :]
            ),
            sends,
            [VM] * (8 + len(before)),
        )(*arrived, edge_local, same, own, bound, *before)
        history.append(outgoing)
        coming = exchange(outgoing)
        now, local, edge_local, *base = call(
            functools.partial(field_kernel, number),
            [field, field, edge_field] + [shape(vecs, vecs)] * (number == 2),
            [SM] + [VM] * 13,
            scratch_shapes=scratch,
        )(cols, live_counts, *arrived, local, stored, degree, place, own, bound, *earlier)
        earlier = [begin, now] if number == 0 else [now, now]
        arrived = coming

    gram = call(gram_kernel, shape(vecs, vecs), [VM] * 8)(*arrived, edge_local, same, peak, *base)
    gram = spread(gram, jnp.add, stages[:-1])
    axis, bit = stages[-1]
    other = lax.ppermute(gram, axis, xor_pairs(lax.axis_size(axis), bit))
    now = call(last_kernel, shape(3 * vecs, cells, dtype=BF16), [VM] * 7)(*arrived, local, place, peak)
    root = math.sqrt(cells * sizes[0] * sizes[1])
    return call(functools.partial(encode_kernel, root), shape(1, 1, vecs, cells), [VM] * 3)(gram, other, now)


def solution(mesh):
    in_specs = (
        P("gx", "gy", None, None),
        P("gx", "gy", None, None, None, None),
        P("gx", "gy", None, None),
        P("gx", "gy", None, None),
        P("gx", "gy"),
    )
    out_specs = P("gx", "gy", None, None)

    return jax.shard_map(
        per_device, mesh=mesh, in_specs=in_specs, out_specs=out_specs, check_vma=False
    )
```

```python
import functools
import math

import jax
import jax.numpy as jnp
from jax import lax
from jax.experimental import pallas as pl
from jax.experimental.pallas import tpu as pltpu
from jax.sharding import PartitionSpec as P


LOWER_FRACTION = 0.125
LANES = 128
CHUNK = 256
F32 = jnp.float32
BF16 = jnp.bfloat16
NT = (((1,), (1,)), ((), ()))
VM = pl.BlockSpec(memory_space=pltpu.VMEM)
SM = pl.BlockSpec(memory_space=pltpu.SMEM)
HBM = pl.BlockSpec(memory_space=pltpu.HBM)
LIMIT = 24 << 20
SIDES = (("gx", 1), ("gy", 1), ("gy", 0), ("gx", 0))


def split(x):
    hi = x.astype(BF16)
    return hi, (x - hi.astype(F32)).astype(BF16)


def stacked(x):
    return jnp.concatenate(split(x), axis=0)


def folded(x):
    half = x.shape[0] // 2
    return x[:half] + x[half:]


def dot(a, b):
    return jnp.dot(a, b, preferred_element_type=F32)


def dot_nt(a, b):
    return lax.dot_general(a, b, NT, preferred_element_type=F32)


def product_nt(a, b):
    left, right = stacked(a), stacked(b)
    product = folded(dot_nt(left, right))
    half = product.shape[1] // 2
    return product[:, :half] + product[:, half:]


def total(terms):
    terms = list(terms)
    while len(terms) > 1:
        terms = [a + b for a, b in zip(terms[::2], terms[1::2])] + terms[len(terms) & ~1 :]
    return terms[0]


def near_pairs(size):
    return [(i, i ^ 1) for i in range(size)]


def far_pairs(size):
    return [(i, (i + 1 if i % 2 else i - 1) % size) for i in range(size)]


def turn_pairs(size):
    up = [(i, i + 2 if i + 2 < size else i + 1) for i in range(0, size, 2)]
    down = [(i, i - 2 if i > 1 else 0) for i in range(1, size, 2)]
    return up + down


def xor_pairs(size, bit):
    return [(i, i ^ bit) for i in range(size)]


def live_lanes(count, start, width):
    return lax.broadcasted_iota(jnp.int32, (1, width), 1) + start < count


def left_rows(value):
    hi, lo = split(value)
    return jnp.concatenate(
        [
            jnp.concatenate([hi, hi], axis=1),
            jnp.concatenate([lo, jnp.zeros_like(lo)], axis=1),
        ],
        axis=0,
    )


def scalars(peak):
    upper = 2.0 * peak[0:1, 0:1]
    lower = LOWER_FRACTION * upper
    return (upper + lower) / 2.0, (upper - lower) / 2.0


def first_kernel(sizes, cols, counts, lists_any, basis_any, weights_any, *refs):
    place, stored, begin, degree, peak, marks = refs[:6]
    outs = refs[6:10]
    lists, basis, weights, hits, sems = refs[10:]
    blocks, slots = weights.shape[:2]
    cells, edges = place.shape
    width = edges // len(outs)
    loads = [
        pltpu.make_async_copy(lists_any.at[0, 0], lists, sems.at[blocks]),
        pltpu.make_async_copy(basis_any.at[0, 0], basis, sems.at[blocks + 1]),
    ]
    blocks_in = [
        pltpu.make_async_copy(weights_any.at[0, 0, m], weights.at[m], sems.at[m]) for m in range(blocks)
    ]
    for load in loads:
        load.start()
    count = counts[...]
    degree[...] = jnp.zeros_like(degree)
    for load in loads:
        load.wait()
    for load in blocks_in:
        load.start()
    order = []
    for axis, shift in SIDES:
        dim = ("gx", "gy").index(axis)
        me = lax.axis_index(axis)
        upward = me % 2 == shift
        low, high = lists[2 * dim : 2 * dim + 1], lists[2 * dim + 1 : 2 * dim + 2]
        low, high = jnp.where(me > 0, low, -1), jnp.where(me < sizes[dim] - 1, high, -1)
        order.append(jnp.where(upward, high, low))
    targets = jnp.concatenate(order, axis=1)
    marks[...] = jnp.broadcast_to(targets, marks.shape)
    for start in range(0, cells, CHUNK):
        spot = lax.broadcasted_iota(jnp.int32, (CHUNK, edges), 0) + start
        equal = (spot == targets).astype(F32)
        place[start : start + CHUNK] = equal.astype(BF16)
        hits[start : start + CHUNK] = total(
            equal[:, other : other + LANES] for other in range(0, edges, LANES)
        ).astype(BF16)
    begin[...] = jnp.where(live_lanes(count, 0, cells), basis[...], 0.0)
    picked = folded(dot(stacked(begin[...]), place[...]))
    for i, out in enumerate(outs):
        out[...] = picked[:, i * width : (i + 1) * width]
    joined = dot_nt(jnp.ones((16, LANES), BF16), hits[...])[:8]
    rows = lax.broadcasted_iota(jnp.int32, (LANES, LANES), 0)
    for m in range(blocks):
        blocks_in[m].wait()
        live = rows + m * LANES < count
        for j in range(slots):
            value = weights[m, j]
            hi, lo = split(value)
            stored[m, 0:LANES, j * LANES : (j + 1) * LANES] = hi
            stored[m, LANES : 2 * LANES, j * LANES : (j + 1) * LANES] = lo
            kept = jnp.where(live, value, 0.0)
            spot = pl.ds(pl.multiple_of(cols[0, j, 0, m] * LANES, LANES), LANES)
            degree[:, spot] += total(kept[i : i + 8] for i in range(0, LANES, 8))
    value = jnp.sum(degree[...], axis=0, keepdims=True) + joined
    value = jnp.where(live_lanes(count, 0, cells), value, 0.0)
    degree[...] = value
    peak[...] = jnp.full(peak.shape, jnp.max(value), F32)


def multiply(cols, m, value, stored, inside):
    product = folded(dot(left_rows(value), stored[m]))
    for j in range(stored.shape[2] // LANES):
        spot = pl.ds(pl.multiple_of(cols[0, j, 0, m] * LANES, LANES), LANES)
        inside[:, spot] += product[:, j * LANES : (j + 1) * LANES]


def gather(values, place):
    return folded(dot(stacked(values), place[...]))


def joined_up(parts):
    return jnp.concatenate([part[...] for part in parts], axis=1)


def chunks(cells):
    return [slice(start, start + CHUNK) for start in range(0, cells, CHUNK)]


def open_kernel(cols, counts, begin, stored, degree, place, marks, local, edge_local, same, back, inside):
    cells, edges = place.shape
    targets = marks[0:1]
    for start in range(0, edges, LANES):
        across = jnp.broadcast_to(targets[:, start : start + LANES], (LANES, LANES))
        down = across.astype(F32).T.astype(jnp.int32)
        down = jnp.where(down < 0, -2, down)
        for other in range(0, edges, LANES):
            equal = down == targets[:, other : other + LANES]
            same[start : start + LANES, other : other + LANES] = equal.astype(F32).astype(BF16)
        lane = lax.broadcasted_iota(jnp.int32, (LANES, LANES), 1)
        for other in range(0, cells, LANES):
            equal = down == lane + other
            back[start : start + LANES, other : other + LANES] = equal.astype(F32).astype(BF16)
    inside[...] = jnp.zeros_like(inside)
    for m in range(cells // LANES):
        multiply(cols, m, begin[:, m * LANES : (m + 1) * LANES], stored, inside)
    for part in chunks(cells):
        live = live_lanes(counts[...], part.start, CHUNK)
        local[:, part] = degree[0:1, part] * begin[:, part] - jnp.where(live, inside[:, part], 0.0)
    edge_local[...] = gather(local[...], place)


def edges_kernel(number, r0, r1, r2, r3, edge_local, same, own, peak, before, *outs):
    crossed = folded(dot(stacked(joined_up((r0, r1, r2, r3))), same[...]))
    if number == 0:
        value = edge_local[...] - crossed
    elif number == 1:
        centre, half = scalars(peak)
        top = own[0:1, 0:1]
        first, second = joined_up(before[:4]), joined_up(before[4:])
        value = second_field(centre, half, top, edge_local[...] - crossed / top, second, first)[1]
    else:
        _, half = scalars(peak)
        value = edge_local[...] - (2.0 / half) * crossed
    width = value.shape[1] // len(outs)
    for i, out in enumerate(outs):
        out[...] = value[:, i * width : (i + 1) * width]


def second_field(centre, half, top, twice, once, begin):
    ratio = centre / half
    shrunk = once / half
    first = shrunk - ratio * begin
    second = (2.0 / half) * (top / half) * twice - 2.0 * ratio * (shrunk + first) - begin
    return first, second


def field_kernel(
    number, cols, counts, r0, r1, r2, r3, local, stored, degree, place, back, own, peak, begin, once, *refs
):
    field, later, edge_local = refs[:3]
    inside = refs[-1]
    cells = place.shape[0]
    top = own[0:1, 0:1]
    centre, half = scalars(peak)
    arrived = stacked(joined_up((r0, r1, r2, r3)))
    inside[...] = jnp.zeros_like(inside)
    for part in chunks(cells):
        crossed = folded(dot(arrived, back[:, part]))
        if number == 0:
            value = (local[:, part] - crossed) / top
        elif number == 1:
            first, value = second_field(
                centre, half, top, local[:, part] - crossed / top, once[:, part] * top, begin[:, part]
            )
            later[:, part] = first
        else:
            value = local[:, part] - (2.0 / half) * crossed
            later[:, part] = begin[:, part]
        field[:, part] = value
        for start in range(0, CHUNK, LANES):
            block = (part.start + start) // LANES
            multiply(cols, block, value[:, start : start + LANES], stored, inside)
    for part in chunks(cells):
        live = live_lanes(counts[...], part.start, CHUNK)
        kept = jnp.where(live, inside[:, part], 0.0)
        if number == 0:
            later[:, part] = degree[0:1, part] * field[:, part] - kept
        else:
            value = (degree[0:1, part] - centre) * field[:, part] - kept
            later[:, part] = (2.0 / half) * value - later[:, part]
    edge_local[...] = gather(later[...], place)
    if number == 2:
        refs[3][...] = product_nt(later[...], later[...])


def gram_kernel(r0, r1, r2, r3, edge_local, same, peak, base, gram):
    _, half = scalars(peak)
    scale = 2.0 / half
    arrived = joined_up((r0, r1, r2, r3))
    crossed = folded(dot(stacked(arrived), same[...]))
    mixed = product_nt(scale * (edge_local[...] - (0.5 * scale) * crossed), arrived)
    gram[...] = base[...] - mixed - mixed.T


def last_kernel(r0, r1, r2, r3, local, back, peak, terms):
    _, half = scalars(peak)
    arrived = stacked(joined_up((r0, r1, r2, r3)))
    for part in chunks(back.shape[1]):
        hi, lo = split(local[:, part] - (2.0 / half) * folded(dot(arrived, back[:, part])))
        terms[:, part] = jnp.concatenate([hi, lo, hi], axis=0)


def small_inverse(rows, start, size, width):
    near = [
        [jnp.broadcast_to(rows[i : i + 1, start + j : start + j + 1], (size, width)) for j in range(i + 1)]
        for i in range(size)
    ]
    far = [[None] * size for _ in range(size)]
    for k in range(size):
        pivot = near[k][k]
        inverse = 1.0 / pivot
        for i in range(k + 1, size):
            factor = near[i][k] * inverse
            for j in range(k + 1, i + 1):
                near[i][j] = near[i][j] - factor * near[j][k]
            for j in range(k):
                far[i][j] = far[i][j] - factor * far[k][j]
            far[i][k] = -factor
        root = lax.rsqrt(pivot)
        near[k] = root
    return [
        [far[i][j] * near[i] for j in range(i)] + [near[i]] for i in range(size)
    ]


def encode_kernel(root, first, second, values, out):
    gram = first[...] + second[...]
    vecs = gram.shape[0]
    size = 8
    lane = lax.broadcasted_iota(jnp.int32, (size, vecs), 1)
    sub = lax.broadcasted_iota(jnp.int32, (size, vecs), 0)
    rows = [gram[i * size : (i + 1) * size] for i in range(vecs // size)]
    for g in range(vecs // size):
        start = g * size
        inside = jnp.logical_and(lane >= start, lane < start + size)
        small = small_inverse(rows[g], start, size, vecs)
        unit = jnp.where(inside, (lane - start == sub).astype(F32), rows[g])
        spread_rows = [jnp.broadcast_to(unit[j : j + 1], (size, vecs)) for j in range(size)]
        half = [
            total(small[i][j] * spread_rows[j] for j in range(i + 1)) for i in range(size)
        ]
        whole = [
            total(small[i][j] * half[i] for i in range(j, size)) for j in range(size)
        ]
        for i in range(g + 1, vecs // size):
            kept = jnp.where(inside, 0.0, rows[i])
            rows[i] = kept - total(
                jnp.broadcast_to(rows[i][:, start + j : start + j + 1], (size, vecs)) * whole[j]
                for j in range(size)
            )
        done = half[0]
        for j in range(1, size):
            done = jnp.where(sub == j, half[j], done)
        rows[g] = jnp.where(lane < start + size, done, 0.0)
    hi, lo = split(jnp.concatenate(rows, axis=0) * root)
    out[0, 0] = dot(jnp.concatenate([hi, hi, lo], axis=1), values[...])


def call(kernel, shapes, specs, **extra):
    many = isinstance(shapes, (tuple, list))
    return pl.pallas_call(
        kernel,
        out_shape=shapes,
        in_specs=specs,
        out_specs=[VM] * len(shapes) if many else VM,
        compiler_params=pltpu.CompilerParams(vmem_limit_bytes=LIMIT),
        **extra,
    )


def shape(*dims, dtype=F32):
    return jax.ShapeDtypeStruct(dims, dtype)


def spread(value, combine, stages):
    for axis, bit in stages:
        pairs = xor_pairs(lax.axis_size(axis), bit)
        value = combine(value, lax.ppermute(value, axis, pairs))
    return value


def per_device(basis, block_vals, block_cols, edge_rows, live_counts):
    vecs, cells = basis.shape[2:]
    blocks, slots, block = block_vals.shape[2:5]
    edges = edge_rows.shape[3]
    sizes = (lax.axis_size("gx"), lax.axis_size("gy"))
    field = shape(vecs, cells)
    sends = [shape(vecs, edges)] * 4
    edge_field = shape(vecs, 4 * edges)
    scratch = [pltpu.VMEM((vecs, cells), F32)]

    def exchange(parts):
        x_far, y_far, y_near, x_near = parts
        x_far = lax.ppermute(x_far, "gx", near_pairs(sizes[0]))
        y_far = lax.ppermute(y_far, "gy", far_pairs(sizes[1]))
        y_near = lax.ppermute(y_near, "gy", near_pairs(sizes[1]))
        x_far = lax.ppermute(x_far, "gx", turn_pairs(sizes[0]))
        x_near = lax.ppermute(x_near, "gx", near_pairs(sizes[0]))
        return [x_far, y_far, y_near, x_near]

    cols = jnp.transpose(block_cols, (0, 3, 1, 2))
    place, stored, begin, degree, own, marks, *outgoing = call(
        functools.partial(first_kernel, sizes),
        [
            shape(cells, 4 * edges, dtype=BF16),
            shape(blocks, 2 * block, slots * block, dtype=BF16),
            field,
            shape(8, cells),
            shape(8, LANES),
            shape(8, 4 * edges, dtype=jnp.int32),
        ]
        + sends,
        [SM, VM] + [HBM] * 3,
        scratch_shapes=[
            pltpu.VMEM((4, edges), jnp.int32),
            pltpu.VMEM((vecs, cells), F32),
            pltpu.VMEM((blocks, slots, block, block), F32),
            pltpu.VMEM((cells, LANES), BF16),
            pltpu.SemaphoreType.DMA((blocks + 2,)),
        ],
    )(
        cols,
        live_counts,
        *(pltpu.with_memory_space_constraint(x, pltpu.HBM) for x in (edge_rows, basis, block_vals)),
    )
    stages = [
        (axis, 1 << b) for axis, size in zip(("gx", "gy"), sizes) for b in range(size.bit_length() - 1)
    ]
    arrived = exchange(outgoing)
    peak = spread(own, jnp.maximum, stages)
    local, edge_local, same, back = call(
        open_kernel,
        [
            field,
            edge_field,
            shape(4 * edges, 4 * edges, dtype=BF16),
            shape(4 * edges, cells, dtype=BF16),
        ],
        [SM] + [VM] * 6,
        scratch_shapes=scratch,
    )(cols, live_counts, begin, stored, degree, place, marks)

    history, earlier = [outgoing], [begin, begin]
    for number in range(3):
        bound = peak if number else own
        before = [x for parts in history for x in parts] if number == 1 else []
        outgoing = call(
            lambda *refs, number=number, count=len(before): edges_kernel(
                number, *refs[:8], refs[8 : 8 + count], *refs[8 + count :]
            ),
            sends,
            [VM] * (8 + len(before)),
        )(*arrived, edge_local, same, own, bound, *before)
        history.append(outgoing)
        coming = exchange(outgoing)
        now, local, edge_local, *base = call(
            functools.partial(field_kernel, number),
            [field, field, edge_field] + [shape(vecs, vecs)] * (number == 2),
            [SM] + [VM] * 14,
            scratch_shapes=scratch,
        )(cols, live_counts, *arrived, local, stored, degree, place, back, own, bound, *earlier)
        earlier = [begin, now] if number == 0 else [now, now]
        arrived = coming

    gram = call(gram_kernel, shape(vecs, vecs), [VM] * 8)(*arrived, edge_local, same, peak, *base)
    gram = spread(gram, jnp.add, stages[:-1])
    axis, bit = stages[-1]
    other = lax.ppermute(gram, axis, xor_pairs(lax.axis_size(axis), bit))
    now = call(last_kernel, shape(3 * vecs, cells, dtype=BF16), [VM] * 7)(*arrived, local, back, peak)
    root = math.sqrt(cells * sizes[0] * sizes[1])
    return call(functools.partial(encode_kernel, root), shape(1, 1, vecs, cells), [VM] * 3)(gram, other, now)


def solution(mesh):
    in_specs = (
        P("gx", "gy", None, None),
        P("gx", "gy", None, None, None, None),
        P("gx", "gy", None, None),
        P("gx", "gy", None, None),
        P("gx", "gy"),
    )
    out_specs = P("gx", "gy", None, None)

    return jax.shard_map(
        per_device, mesh=mesh, in_specs=in_specs, out_specs=out_specs, check_vma=False
    )
```

```python
import functools
import math

import jax
import jax.numpy as jnp
from jax import lax
from jax.experimental import pallas as pl
from jax.experimental.pallas import tpu as pltpu
from jax.sharding import PartitionSpec as P


LOWER_FRACTION = 0.125
LANES = 128
SHIFT = 7
CHUNK = 256
F32 = jnp.float32
BF16 = jnp.bfloat16
NT = (((1,), (1,)), ((), ()))
VM = pl.BlockSpec(memory_space=pltpu.VMEM)
SM = pl.BlockSpec(memory_space=pltpu.SMEM)
HBM = pl.BlockSpec(memory_space=pltpu.HBM)
LIMIT = 24 << 20
SIDES = (("gx", 1), ("gy", 1), ("gy", 0), ("gx", 0))


def split(x):
    hi = x.astype(BF16)
    return hi, (x - hi.astype(F32)).astype(BF16)


def stacked(x):
    return jnp.concatenate(split(x), axis=0)


def folded(x):
    half = x.shape[0] // 2
    return x[:half] + x[half:]


def dot(a, b):
    return jnp.dot(a, b, preferred_element_type=F32)


def dot_nt(a, b):
    return lax.dot_general(a, b, NT, preferred_element_type=F32)


def product_nt(a, b):
    left, right = stacked(a), stacked(b)
    product = folded(dot_nt(left, right))
    half = product.shape[1] // 2
    return product[:, :half] + product[:, half:]


def total(terms):
    terms = list(terms)
    while len(terms) > 1:
        terms = [a + b for a, b in zip(terms[::2], terms[1::2])] + terms[len(terms) & ~1 :]
    return terms[0]


def near_pairs(size):
    return [(i, i ^ 1) for i in range(size)]


def far_pairs(size):
    return [(i, (i + 1 if i % 2 else i - 1) % size) for i in range(size)]


def turn_pairs(size):
    up = [(i, i + 2 if i + 2 < size else i + 1) for i in range(0, size, 2)]
    down = [(i, i - 2 if i > 1 else 0) for i in range(1, size, 2)]
    return up + down


def xor_pairs(size, bit):
    return [(i, i ^ bit) for i in range(size)]


def live_lanes(count, start, width):
    return lax.broadcasted_iota(jnp.int32, (1, width), 1) + start < count


def left_rows(value):
    hi, lo = split(value)
    return jnp.concatenate(
        [
            jnp.concatenate([hi, hi], axis=1),
            jnp.concatenate([lo, jnp.zeros_like(lo)], axis=1),
        ],
        axis=0,
    )


def scalars(peak):
    upper = 2.0 * peak[0:1, 0:1]
    lower = LOWER_FRACTION * upper
    return (upper + lower) / 2.0, (upper - lower) / 2.0


def first_kernel(sizes, cols, counts, lists_any, basis_any, weights_any, *refs):
    place, stored, begin, degree, peak, marks = refs[:6]
    outs = refs[6:10]
    lists, basis, weights, hits, sems = refs[10:]
    blocks, slots = weights.shape[:2]
    cells, edges = place.shape
    width = edges // len(outs)
    loads = [
        pltpu.make_async_copy(lists_any.at[0, 0], lists, sems.at[blocks]),
        pltpu.make_async_copy(basis_any.at[0, 0], basis, sems.at[blocks + 1]),
    ]
    blocks_in = [
        pltpu.make_async_copy(weights_any.at[0, 0, m], weights.at[m], sems.at[m]) for m in range(blocks)
    ]
    for load in loads:
        load.start()
    count = counts[...]
    degree[...] = jnp.zeros_like(degree)
    for load in loads:
        load.wait()
    for load in blocks_in:
        load.start()
    order = []
    for axis, shift in SIDES:
        dim = ("gx", "gy").index(axis)
        me = lax.axis_index(axis)
        upward = me % 2 == shift
        low, high = lists[2 * dim : 2 * dim + 1], lists[2 * dim + 1 : 2 * dim + 2]
        low, high = jnp.where(me > 0, low, -1), jnp.where(me < sizes[dim] - 1, high, -1)
        order.append(jnp.where(upward, high, low))
    targets = jnp.concatenate(order, axis=1)
    marks[...] = jnp.broadcast_to(targets, marks.shape)
    spot = lax.broadcasted_iota(jnp.int32, (LANES, edges), 0)
    within = (spot == (targets & (LANES - 1))).astype(F32).astype(BF16)
    block = jnp.broadcast_to((targets >> SHIFT).astype(F32).astype(BF16), within.shape)
    for m in range(blocks):
        equal = jnp.where(block == BF16(m), within, jnp.zeros_like(within))
        place[m * LANES : (m + 1) * LANES] = equal
        hits[m * LANES : (m + 1) * LANES] = total(
            equal[:, other : other + LANES] for other in range(0, edges, LANES)
        )
    begin[...] = jnp.where(live_lanes(count, 0, cells), basis[...], 0.0)
    picked = folded(dot(stacked(begin[...]), place[...]))
    for i, out in enumerate(outs):
        out[...] = picked[:, i * width : (i + 1) * width]
    joined = dot_nt(jnp.ones((16, LANES), BF16), hits[...])[:8]
    rows = lax.broadcasted_iota(jnp.int32, (LANES, LANES), 0)
    for m in range(blocks):
        blocks_in[m].wait()
        live = rows + m * LANES < count
        for j in range(slots):
            value = weights[m, j]
            hi, lo = split(value)
            stored[m, 0:LANES, j * LANES : (j + 1) * LANES] = hi
            stored[m, LANES : 2 * LANES, j * LANES : (j + 1) * LANES] = lo
            kept = jnp.where(live, value, 0.0)
            spot = pl.ds(pl.multiple_of(cols[0, j, 0, m] * LANES, LANES), LANES)
            degree[:, spot] += total(kept[i : i + 8] for i in range(0, LANES, 8))
    value = jnp.sum(degree[...], axis=0, keepdims=True) + joined
    value = jnp.where(live_lanes(count, 0, cells), value, 0.0)
    degree[...] = value
    peak[...] = jnp.full(peak.shape, jnp.max(value), F32)


def multiply(cols, values, stored, inside):
    blocks, _, width = stored.shape
    inside[...] = jnp.zeros_like(inside)
    for m in range(blocks):
        product = folded(dot(left_rows(values[:, m * LANES : (m + 1) * LANES]), stored[m]))
        for j in range(width // LANES):
            spot = pl.ds(pl.multiple_of(cols[0, j, 0, m] * LANES, LANES), LANES)
            inside[:, spot] += product[:, j * LANES : (j + 1) * LANES]


def gather(values, place):
    return folded(dot(stacked(values), place[...]))


def joined_up(parts):
    return jnp.concatenate([part[...] for part in parts], axis=1)


def chunks(cells):
    return [slice(start, start + CHUNK) for start in range(0, cells, CHUNK)]


def open_kernel(cols, counts, begin, stored, degree, place, marks, local, edge_local, same, back, inside):
    cells, edges = place.shape
    targets = marks[0:1]
    for start in range(0, edges, LANES):
        across = jnp.broadcast_to(targets[:, start : start + LANES], (LANES, LANES))
        down = across.astype(F32).T.astype(jnp.int32)
        down = jnp.where(down < 0, -2, down)
        for other in range(0, edges, LANES):
            equal = down == targets[:, other : other + LANES]
            same[start : start + LANES, other : other + LANES] = equal.astype(F32).astype(BF16)
        lane = lax.broadcasted_iota(jnp.int32, (LANES, LANES), 1)
        within = ((down & (LANES - 1)) == lane).astype(F32).astype(BF16)
        block = (down >> SHIFT).astype(F32).astype(BF16)
        for m in range(cells // LANES):
            equal = jnp.where(block == BF16(m), within, jnp.zeros_like(within))
            back[start : start + LANES, m * LANES : (m + 1) * LANES] = equal
    multiply(cols, begin, stored, inside)
    for part in chunks(cells):
        live = live_lanes(counts[...], part.start, CHUNK)
        local[:, part] = degree[0:1, part] * begin[:, part] - jnp.where(live, inside[:, part], 0.0)
    edge_local[...] = gather(local[...], place)


def edges_kernel(number, r0, r1, r2, r3, edge_local, same, own, peak, before, *outs):
    crossed = folded(dot(stacked(joined_up((r0, r1, r2, r3))), same[...]))
    if number == 0:
        value = edge_local[...] - crossed
    elif number == 1:
        centre, half = scalars(peak)
        top = own[0:1, 0:1]
        first, second = joined_up(before[:4]), joined_up(before[4:])
        value = second_field(centre, half, top, edge_local[...] - crossed / top, second, first)[1]
    else:
        _, half = scalars(peak)
        value = edge_local[...] - (2.0 / half) * crossed
    width = value.shape[1] // len(outs)
    for i, out in enumerate(outs):
        out[...] = value[:, i * width : (i + 1) * width]


def second_field(centre, half, top, twice, once, begin):
    ratio = centre / half
    shrunk = once / half
    first = shrunk - ratio * begin
    second = (2.0 / half) * (top / half) * twice - 2.0 * ratio * (shrunk + first) - begin
    return first, second


def field_kernel(
    number, cols, counts, r0, r1, r2, r3, local, stored, degree, place, back, own, peak, begin, once, *refs
):
    field, later, edge_local = refs[:3]
    inside = refs[-1]
    cells = place.shape[0]
    top = own[0:1, 0:1]
    centre, half = scalars(peak)
    arrived = stacked(joined_up((r0, r1, r2, r3)))
    for part in chunks(cells):
        crossed = folded(dot(arrived, back[:, part]))
        if number == 0:
            value = (local[:, part] - crossed) / top
        elif number == 1:
            first, value = second_field(
                centre, half, top, local[:, part] - crossed / top, once[:, part] * top, begin[:, part]
            )
            later[:, part] = first
        else:
            value = local[:, part] - (2.0 / half) * crossed
            later[:, part] = begin[:, part]
        field[:, part] = value
    multiply(cols, field, stored, inside)
    for part in chunks(cells):
        live = live_lanes(counts[...], part.start, CHUNK)
        kept = jnp.where(live, inside[:, part], 0.0)
        if number == 0:
            later[:, part] = degree[0:1, part] * field[:, part] - kept
        else:
            value = (degree[0:1, part] - centre) * field[:, part] - kept
            later[:, part] = (2.0 / half) * value - later[:, part]
    edge_local[...] = gather(later[...], place)
    if number == 2:
        refs[3][...] = product_nt(later[...], later[...])


def places(size):
    row = lax.broadcasted_iota(jnp.int32, (size, size), 0)
    return row, lax.broadcasted_iota(jnp.int32, (size, size), 1)


def packed(gram):
    size = gram.shape[0] // 2
    row, col = places(size)
    low, high = gram[:size, :size], gram[size:, size:]
    diagonal = jnp.sum(jnp.where(row == col, high, 0.0), axis=1, keepdims=True)
    width = LANES - 2 * size
    return jnp.concatenate(
        [jnp.where(col <= row, low, high), gram[:size, size:], jnp.broadcast_to(diagonal, (size, width))],
        axis=1,
    )


def unpacked(value):
    size = value.shape[0]
    row, col = places(size)
    mixed, cross = value[:, :size], value[:, size : 2 * size]
    below, above = jnp.where(col < row, mixed, 0.0), jnp.where(col > row, mixed, 0.0)
    diagonal = jnp.where(row == col, value[:, 2 * size : 2 * size + 1], 0.0)
    low = jnp.where(row == col, mixed, below) + below.T
    high = above + above.T + diagonal
    return jnp.concatenate(
        [jnp.concatenate([low, cross], axis=1), jnp.concatenate([cross.T, high], axis=1)], axis=0
    )


def gram_kernel(r0, r1, r2, r3, edge_local, same, peak, base, gram):
    _, half = scalars(peak)
    scale = 2.0 / half
    arrived = joined_up((r0, r1, r2, r3))
    crossed = folded(dot(stacked(arrived), same[...]))
    mixed = product_nt(scale * (edge_local[...] - (0.5 * scale) * crossed), arrived)
    gram[...] = packed(base[...] - mixed - mixed.T)


def last_kernel(r0, r1, r2, r3, local, back, peak, terms):
    _, half = scalars(peak)
    arrived = stacked(joined_up((r0, r1, r2, r3)))
    for part in chunks(back.shape[1]):
        hi, lo = split(local[:, part] - (2.0 / half) * folded(dot(arrived, back[:, part])))
        terms[:, part] = jnp.concatenate([hi, lo, hi], axis=0)


def small_inverse(rows, start, size, width):
    near = [
        [jnp.broadcast_to(rows[i : i + 1, start + j : start + j + 1], (size, width)) for j in range(i + 1)]
        for i in range(size)
    ]
    far = [[None] * size for _ in range(size)]
    for k in range(size):
        pivot = near[k][k]
        inverse = 1.0 / pivot
        for i in range(k + 1, size):
            factor = near[i][k] * inverse
            for j in range(k + 1, i + 1):
                near[i][j] = near[i][j] - factor * near[j][k]
            for j in range(k):
                far[i][j] = far[i][j] - factor * far[k][j]
            far[i][k] = -factor
        root = lax.rsqrt(pivot)
        near[k] = root
    return [
        [far[i][j] * near[i] for j in range(i)] + [near[i]] for i in range(size)
    ]


def encode_kernel(root, *refs):
    *parts, values, out = refs
    gram = unpacked(total(part[...] for part in parts))
    vecs = gram.shape[0]
    size = 8
    lane = lax.broadcasted_iota(jnp.int32, (size, vecs), 1)
    sub = lax.broadcasted_iota(jnp.int32, (size, vecs), 0)
    rows = [gram[i * size : (i + 1) * size] for i in range(vecs // size)]
    for g in range(vecs // size):
        start = g * size
        inside = jnp.logical_and(lane >= start, lane < start + size)
        small = small_inverse(rows[g], start, size, vecs)
        unit = jnp.where(inside, (lane - start == sub).astype(F32), rows[g])
        spread_rows = [jnp.broadcast_to(unit[j : j + 1], (size, vecs)) for j in range(size)]
        half = [
            total(small[i][j] * spread_rows[j] for j in range(i + 1)) for i in range(size)
        ]
        whole = [
            total(small[i][j] * half[i] for i in range(j, size)) for j in range(size)
        ]
        for i in range(g + 1, vecs // size):
            kept = jnp.where(inside, 0.0, rows[i])
            rows[i] = kept - total(
                jnp.broadcast_to(rows[i][:, start + j : start + j + 1], (size, vecs)) * whole[j]
                for j in range(size)
            )
        done = half[0]
        for j in range(1, size):
            done = jnp.where(sub == j, half[j], done)
        rows[g] = jnp.where(lane < start + size, done, 0.0)
    hi, lo = split(jnp.concatenate(rows, axis=0) * root)
    out[0, 0] = dot(jnp.concatenate([hi, hi, lo], axis=1), values[...])


def call(kernel, shapes, specs, **extra):
    many = isinstance(shapes, (tuple, list))
    return pl.pallas_call(
        kernel,
        out_shape=shapes,
        in_specs=specs,
        out_specs=[VM] * len(shapes) if many else VM,
        compiler_params=pltpu.CompilerParams(vmem_limit_bytes=LIMIT),
        **extra,
    )


def shape(*dims, dtype=F32):
    return jax.ShapeDtypeStruct(dims, dtype)


def spread(value, combine, stages):
    for axis, bit in stages:
        pairs = xor_pairs(lax.axis_size(axis), bit)
        value = combine(value, lax.ppermute(value, axis, pairs))
    return value


def per_device(basis, block_vals, block_cols, edge_rows, live_counts):
    vecs, cells = basis.shape[2:]
    blocks, slots, block = block_vals.shape[2:5]
    edges = edge_rows.shape[3]
    sizes = (lax.axis_size("gx"), lax.axis_size("gy"))
    field = shape(vecs, cells)
    sends = [shape(vecs, edges)] * 4
    edge_field = shape(vecs, 4 * edges)
    scratch = [pltpu.VMEM((vecs, cells), F32)]

    def exchange(parts):
        x_far, y_far, y_near, x_near = parts
        x_far = lax.ppermute(x_far, "gx", near_pairs(sizes[0]))
        y_far = lax.ppermute(y_far, "gy", far_pairs(sizes[1]))
        y_near = lax.ppermute(y_near, "gy", near_pairs(sizes[1]))
        x_far = lax.ppermute(x_far, "gx", turn_pairs(sizes[0]))
        x_near = lax.ppermute(x_near, "gx", near_pairs(sizes[0]))
        return [x_far, y_far, y_near, x_near]

    cols = jnp.transpose(block_cols, (0, 3, 1, 2))
    place, stored, begin, degree, own, marks, *outgoing = call(
        functools.partial(first_kernel, sizes),
        [
            shape(cells, 4 * edges, dtype=BF16),
            shape(blocks, 2 * block, slots * block, dtype=BF16),
            field,
            shape(8, cells),
            shape(8, LANES),
            shape(8, 4 * edges, dtype=jnp.int32),
        ]
        + sends,
        [SM, VM] + [HBM] * 3,
        scratch_shapes=[
            pltpu.VMEM((4, edges), jnp.int32),
            pltpu.VMEM((vecs, cells), F32),
            pltpu.VMEM((blocks, slots, block, block), F32),
            pltpu.VMEM((cells, LANES), BF16),
            pltpu.SemaphoreType.DMA((blocks + 2,)),
        ],
    )(
        cols,
        live_counts,
        *(pltpu.with_memory_space_constraint(x, pltpu.HBM) for x in (edge_rows, basis, block_vals)),
    )
    stages = [
        (axis, 1 << b) for axis, size in zip(("gx", "gy"), sizes) for b in range(size.bit_length() - 1)
    ]
    arrived = exchange(outgoing)
    peak = spread(own, jnp.maximum, stages)
    local, edge_local, same, back = call(
        open_kernel,
        [
            field,
            edge_field,
            shape(4 * edges, 4 * edges, dtype=BF16),
            shape(4 * edges, cells, dtype=BF16),
        ],
        [SM] + [VM] * 6,
        scratch_shapes=scratch,
    )(cols, live_counts, begin, stored, degree, place, marks)

    history, earlier = [outgoing], [begin, begin]
    for number in range(3):
        bound = peak if number else own
        before = [x for parts in history for x in parts] if number == 1 else []
        outgoing = call(
            lambda *refs, number=number, count=len(before): edges_kernel(
                number, *refs[:8], refs[8 : 8 + count], *refs[8 + count :]
            ),
            sends,
            [VM] * (8 + len(before)),
        )(*arrived, edge_local, same, own, bound, *before)
        history.append(outgoing)
        coming = exchange(outgoing)
        now, local, edge_local, *base = call(
            functools.partial(field_kernel, number),
            [field, field, edge_field] + [shape(vecs, vecs)] * (number == 2),
            [SM] + [VM] * 14,
            scratch_shapes=scratch,
        )(cols, live_counts, *arrived, local, stored, degree, place, back, own, bound, *earlier)
        earlier = [begin, now] if number == 0 else [now, now]
        arrived = coming

    gram = call(gram_kernel, shape(vecs // 2, LANES), [VM] * 8)(*arrived, edge_local, same, peak, *base)
    direct = sizes[1] == 4
    gram = spread(gram, jnp.add, [stage for stage in stages if not (direct and stage[0] == "gy")])
    parts = [gram]
    if direct:
        parts += [lax.ppermute(gram, "gy", xor_pairs(4, bit)) for bit in (3, 2, 1)]
    now = call(last_kernel, shape(3 * vecs, cells, dtype=BF16), [VM] * 7)(*arrived, local, back, peak)
    root = math.sqrt(cells * sizes[0] * sizes[1])
    return call(functools.partial(encode_kernel, root), shape(1, 1, vecs, cells), [VM] * (len(parts) + 1))(
        *parts, now
    )


def solution(mesh):
    in_specs = (
        P("gx", "gy", None, None),
        P("gx", "gy", None, None, None, None),
        P("gx", "gy", None, None),
        P("gx", "gy", None, None),
        P("gx", "gy"),
    )
    out_specs = P("gx", "gy", None, None)

    return jax.shard_map(per_device, mesh=mesh, in_specs=in_specs, out_specs=out_specs, check_vma=False)
```

```python
import functools
import math

import jax
import jax.numpy as jnp
from jax import lax
from jax.experimental import pallas as pl
from jax.experimental.pallas import tpu as pltpu
from jax.sharding import PartitionSpec as P


LOWER_FRACTION = 0.125
LANES = 128
SHIFT = 7
CHUNK = 256
F32 = jnp.float32
BF16 = jnp.bfloat16
NT = (((1,), (1,)), ((), ()))
VM = pl.BlockSpec(memory_space=pltpu.VMEM)
SM = pl.BlockSpec(memory_space=pltpu.SMEM)
HBM = pl.BlockSpec(memory_space=pltpu.HBM)
LIMIT = 24 << 20
SIDES = (("gx", 1), ("gy", 1), ("gy", 0), ("gx", 0))


def split(x):
    hi = x.astype(BF16)
    return hi, (x - hi.astype(F32)).astype(BF16)


def stacked(x):
    return jnp.concatenate(split(x), axis=0)


def folded(x):
    half = x.shape[0] // 2
    return x[:half] + x[half:]


def dot(a, b):
    return jnp.dot(a, b, preferred_element_type=F32)


def dot_nt(a, b):
    return lax.dot_general(a, b, NT, preferred_element_type=F32)


def product_nt(a, b):
    left, right = stacked(a), stacked(b)
    product = folded(dot_nt(left, right))
    half = product.shape[1] // 2
    return product[:, :half] + product[:, half:]


def total(terms):
    terms = list(terms)
    while len(terms) > 1:
        terms = [a + b for a, b in zip(terms[::2], terms[1::2])] + terms[len(terms) & ~1 :]
    return terms[0]


def near_pairs(size):
    return [(i, i ^ 1) for i in range(size)]


def far_pairs(size):
    return [(i, (i + 1 if i % 2 else i - 1) % size) for i in range(size)]


def turn_pairs(size):
    up = [(i, i + 2 if i + 2 < size else i + 1) for i in range(0, size, 2)]
    down = [(i, i - 2 if i > 1 else 0) for i in range(1, size, 2)]
    return up + down


def xor_pairs(size, bit):
    return [(i, i ^ bit) for i in range(size)]


def live_lanes(count, start, width):
    return lax.broadcasted_iota(jnp.int32, (1, width), 1) + start < count


def left_rows(value):
    hi, lo = split(value)
    return jnp.concatenate(
        [
            jnp.concatenate([hi, hi], axis=1),
            jnp.concatenate([lo, jnp.zeros_like(lo)], axis=1),
        ],
        axis=0,
    )


def scalars(peak):
    upper = 2.0 * peak[0:1, 0:1]
    lower = LOWER_FRACTION * upper
    return (upper + lower) / 2.0, (upper - lower) / 2.0


def first_kernel(sizes, cols, counts, lists_any, basis_any, weights_any, *refs):
    place, stored, begin, degree, peak, marks = refs[:6]
    outs = refs[6:10]
    lists, basis, weights, hits, sems = refs[10:]
    blocks, slots = weights.shape[:2]
    cells, edges = place.shape
    width = edges // len(outs)
    loads = [
        pltpu.make_async_copy(lists_any.at[0, 0], lists, sems.at[blocks]),
        pltpu.make_async_copy(basis_any.at[0, 0], basis, sems.at[blocks + 1]),
    ]
    blocks_in = [
        pltpu.make_async_copy(weights_any.at[0, 0, m], weights.at[m], sems.at[m]) for m in range(blocks)
    ]
    for load in loads:
        load.start()
    count = counts[...]
    degree[...] = jnp.zeros_like(degree)
    for load in loads:
        load.wait()
    for load in blocks_in:
        load.start()
    order = []
    for axis, shift in SIDES:
        dim = ("gx", "gy").index(axis)
        me = lax.axis_index(axis)
        upward = me % 2 == shift
        low, high = lists[2 * dim : 2 * dim + 1], lists[2 * dim + 1 : 2 * dim + 2]
        low, high = jnp.where(me > 0, low, -1), jnp.where(me < sizes[dim] - 1, high, -1)
        order.append(jnp.where(upward, high, low))
    targets = jnp.concatenate(order, axis=1)
    marks[...] = jnp.broadcast_to(targets, marks.shape)
    spot = lax.broadcasted_iota(jnp.int32, (LANES, edges), 0)
    within = (spot == (targets & (LANES - 1))).astype(F32).astype(BF16)
    block = jnp.broadcast_to((targets >> SHIFT).astype(F32).astype(BF16), within.shape)
    for m in range(blocks):
        equal = jnp.where(block == BF16(m), within, jnp.zeros_like(within))
        place[m * LANES : (m + 1) * LANES] = equal
        hits[m * LANES : (m + 1) * LANES] = total(
            equal[:, other : other + LANES] for other in range(0, edges, LANES)
        )
    begin[...] = jnp.where(live_lanes(count, 0, cells), basis[...], 0.0)
    picked = folded(dot(stacked(begin[...]), place[...]))
    for i, out in enumerate(outs):
        out[...] = picked[:, i * width : (i + 1) * width]
    joined = dot_nt(jnp.ones((16, LANES), BF16), hits[...])[:8]
    rows = lax.broadcasted_iota(jnp.int32, (LANES, LANES), 0)
    for m in range(blocks):
        blocks_in[m].wait()
        live = rows + m * LANES < count
        for j in range(slots):
            value = weights[m, j]
            hi, lo = split(value)
            stored[m, 0:LANES, j * LANES : (j + 1) * LANES] = hi
            stored[m, LANES : 2 * LANES, j * LANES : (j + 1) * LANES] = lo
            kept = jnp.where(live, value, 0.0)
            spot = pl.ds(pl.multiple_of(cols[0, j, 0, m] * LANES, LANES), LANES)
            degree[:, spot] += total(kept[i : i + 8] for i in range(0, LANES, 8))
    value = jnp.sum(degree[...], axis=0, keepdims=True) + joined
    value = jnp.where(live_lanes(count, 0, cells), value, 0.0)
    degree[...] = value
    peak[...] = jnp.full(peak.shape, jnp.max(value), F32)


def multiply(cols, values, stored, inside):
    blocks, _, width = stored.shape
    inside[...] = jnp.zeros_like(inside)
    for m in range(blocks):
        product = folded(dot(left_rows(values[:, m * LANES : (m + 1) * LANES]), stored[m]))
        for j in range(width // LANES):
            spot = pl.ds(pl.multiple_of(cols[0, j, 0, m] * LANES, LANES), LANES)
            inside[:, spot] += product[:, j * LANES : (j + 1) * LANES]


def gather(values, place):
    return folded(dot(stacked(values), place[...]))


def joined_up(parts):
    return jnp.concatenate([part[...] for part in parts], axis=1)


def chunks(cells):
    return [slice(start, start + CHUNK) for start in range(0, cells, CHUNK)]


def open_kernel(cols, counts, begin, stored, degree, place, marks, local, edge_local, same, back, inside):
    cells, edges = place.shape
    targets = marks[0:1]
    for start in range(0, edges, LANES):
        across = jnp.broadcast_to(targets[:, start : start + LANES], (LANES, LANES))
        down = across.astype(F32).T.astype(jnp.int32)
        down = jnp.where(down < 0, -2, down)
        for other in range(0, edges, LANES):
            equal = down == targets[:, other : other + LANES]
            same[start : start + LANES, other : other + LANES] = equal.astype(F32).astype(BF16)
        lane = lax.broadcasted_iota(jnp.int32, (LANES, LANES), 1)
        within = ((down & (LANES - 1)) == lane).astype(F32).astype(BF16)
        block = (down >> SHIFT).astype(F32).astype(BF16)
        for m in range(cells // LANES):
            equal = jnp.where(block == BF16(m), within, jnp.zeros_like(within))
            back[start : start + LANES, m * LANES : (m + 1) * LANES] = equal
    multiply(cols, begin, stored, inside)
    for part in chunks(cells):
        live = live_lanes(counts[...], part.start, CHUNK)
        local[:, part] = degree[0:1, part] * begin[:, part] - jnp.where(live, inside[:, part], 0.0)
    edge_local[...] = gather(local[...], place)


def edges_kernel(number, r0, r1, r2, r3, edge_local, same, own, peak, before, *outs):
    crossed = folded(dot(stacked(joined_up((r0, r1, r2, r3))), same[...]))
    if number == 0:
        value = edge_local[...] - crossed
    elif number == 1:
        centre, half = scalars(peak)
        top = own[0:1, 0:1]
        first, second = joined_up(before[:4]), joined_up(before[4:])
        value = second_field(centre, half, top, edge_local[...] - crossed / top, second, first)[1]
    else:
        _, half = scalars(peak)
        value = edge_local[...] - (2.0 / half) * crossed
    width = value.shape[1] // len(outs)
    for i, out in enumerate(outs):
        out[...] = value[:, i * width : (i + 1) * width]


def second_field(centre, half, top, twice, once, begin):
    ratio = centre / half
    shrunk = once / half
    first = shrunk - ratio * begin
    second = (2.0 / half) * (top / half) * twice - 2.0 * ratio * (shrunk + first) - begin
    return first, second


def field_kernel(
    number, cols, counts, r0, r1, r2, r3, local, stored, degree, place, back, own, peak, begin, once, *refs
):
    field, later, edge_local = refs[:3]
    inside = refs[-1]
    cells = place.shape[0]
    top = own[0:1, 0:1]
    centre, half = scalars(peak)
    arrived = stacked(joined_up((r0, r1, r2, r3)))
    for part in chunks(cells):
        crossed = folded(dot(arrived, back[:, part]))
        if number == 0:
            value = (local[:, part] - crossed) / top
        elif number == 1:
            first, value = second_field(
                centre, half, top, local[:, part] - crossed / top, once[:, part] * top, begin[:, part]
            )
            later[:, part] = first
        else:
            value = local[:, part] - (2.0 / half) * crossed
            later[:, part] = begin[:, part]
        field[:, part] = value
    multiply(cols, field, stored, inside)
    for part in chunks(cells):
        live = live_lanes(counts[...], part.start, CHUNK)
        kept = jnp.where(live, inside[:, part], 0.0)
        if number == 0:
            later[:, part] = degree[0:1, part] * field[:, part] - kept
        else:
            value = (degree[0:1, part] - centre) * field[:, part] - kept
            later[:, part] = (2.0 / half) * value - later[:, part]
    edge_local[...] = gather(later[...], place)
    if number == 2:
        refs[3][...] = product_nt(later[...], later[...])


def places(size):
    row = lax.broadcasted_iota(jnp.int32, (size, size), 0)
    return row, lax.broadcasted_iota(jnp.int32, (size, size), 1)


def packed(gram):
    size = gram.shape[0] // 2
    row, col = places(size)
    low, high = gram[:size, :size], gram[size:, size:]
    diagonal = jnp.sum(jnp.where(row == col, high, 0.0), axis=1, keepdims=True)
    width = LANES - 2 * size
    return jnp.concatenate(
        [jnp.where(col <= row, low, high), gram[:size, size:], jnp.broadcast_to(diagonal, (size, width))],
        axis=1,
    )


def unpacked(value):
    size = value.shape[0]
    row, col = places(size)
    mixed, cross = value[:, :size], value[:, size : 2 * size]
    below, above = jnp.where(col < row, mixed, 0.0), jnp.where(col > row, mixed, 0.0)
    diagonal = jnp.where(row == col, value[:, 2 * size : 2 * size + 1], 0.0)
    low = jnp.where(row == col, mixed, below) + below.T
    high = above + above.T + diagonal
    return jnp.concatenate(
        [jnp.concatenate([low, cross], axis=1), jnp.concatenate([cross.T, high], axis=1)], axis=0
    )


def gram_kernel(r0, r1, r2, r3, edge_local, same, peak, base, gram):
    _, half = scalars(peak)
    scale = 2.0 / half
    arrived = joined_up((r0, r1, r2, r3))
    crossed = folded(dot(stacked(arrived), same[...]))
    mixed = product_nt(scale * (edge_local[...] - (0.5 * scale) * crossed), arrived)
    gram[...] = packed(base[...] - mixed - mixed.T)


def last_kernel(r0, r1, r2, r3, local, back, peak, terms):
    _, half = scalars(peak)
    arrived = stacked(joined_up((r0, r1, r2, r3)))
    for part in chunks(back.shape[1]):
        hi, lo = split(local[:, part] - (2.0 / half) * folded(dot(arrived, back[:, part])))
        terms[:, part] = jnp.concatenate([hi, lo, hi], axis=0)


def eliminate(block, start, right):
    size, width = block.shape
    near = [
        [jnp.broadcast_to(block[i : i + 1, start + j : start + j + 1], (size, width)) for j in range(i + 1)]
        for i in range(size)
    ]
    rows, factors, inverses = list(right), [[] for _ in range(size)], []
    for k in range(size):
        inverses.append(1.0 / near[k][k])
        for i in range(k + 1, size):
            factor = near[i][k] * inverses[k]
            factors[i].append(factor)
            for j in range(k + 1, i + 1):
                near[i][j] = near[i][j] - factor * near[j][k]
            rows[i] = rows[i] - factor * rows[k]
    half = [lax.rsqrt(near[i][i]) * rows[i] for i in range(size)]
    whole = [rows[i] * inverses[i] for i in range(size)]
    for i in reversed(range(size)):
        for j in range(i):
            whole[j] = whole[j] - factors[i][j] * whole[i]
    return half, whole


def encode_kernel(root, *refs):
    *parts, values, out = refs
    gram = unpacked(total(part[...] for part in parts))
    vecs = gram.shape[0]
    size = 8
    lane = lax.broadcasted_iota(jnp.int32, (size, vecs), 1)
    sub = lax.broadcasted_iota(jnp.int32, (size, vecs), 0)
    rows = [gram[i * size : (i + 1) * size] for i in range(vecs // size)]
    for g in range(vecs // size):
        start = g * size
        inside = jnp.logical_and(lane >= start, lane < start + size)
        unit = jnp.where(inside, (lane - start == sub).astype(F32), rows[g])
        spread_rows = [jnp.broadcast_to(unit[j : j + 1], (size, vecs)) for j in range(size)]
        half, whole = eliminate(rows[g], start, spread_rows)
        for i in range(g + 1, vecs // size):
            kept = jnp.where(inside, 0.0, rows[i])
            rows[i] = kept - total(
                jnp.broadcast_to(rows[i][:, start + j : start + j + 1], (size, vecs)) * whole[j]
                for j in range(size)
            )
        done = half[0]
        for j in range(1, size):
            done = jnp.where(sub == j, half[j], done)
        rows[g] = jnp.where(lane < start + size, done, 0.0)
    hi, lo = split(jnp.concatenate(rows, axis=0) * root)
    out[0, 0] = dot(jnp.concatenate([hi, hi, lo], axis=1), values[...])


def call(kernel, shapes, specs, **extra):
    many = isinstance(shapes, (tuple, list))
    return pl.pallas_call(
        kernel,
        out_shape=shapes,
        in_specs=specs,
        out_specs=[VM] * len(shapes) if many else VM,
        compiler_params=pltpu.CompilerParams(vmem_limit_bytes=LIMIT),
        **extra,
    )


def shape(*dims, dtype=F32):
    return jax.ShapeDtypeStruct(dims, dtype)


def spread(value, combine, stages):
    for axis, bit in stages:
        pairs = xor_pairs(lax.axis_size(axis), bit)
        value = combine(value, lax.ppermute(value, axis, pairs))
    return value


def all_of(value, axis, bits):
    size = lax.axis_size(axis)
    return [value] + [lax.ppermute(value, axis, xor_pairs(size, bit)) for bit in bits]


def per_device(basis, block_vals, block_cols, edge_rows, live_counts):
    vecs, cells = basis.shape[2:]
    blocks, slots, block = block_vals.shape[2:5]
    edges = edge_rows.shape[3]
    sizes = (lax.axis_size("gx"), lax.axis_size("gy"))
    field = shape(vecs, cells)
    sends = [shape(vecs, edges)] * 4
    edge_field = shape(vecs, 4 * edges)
    scratch = [pltpu.VMEM((vecs, cells), F32)]

    def exchange(parts):
        x_far, y_far, y_near, x_near = parts
        x_far = lax.ppermute(x_far, "gx", near_pairs(sizes[0]))
        y_far = lax.ppermute(y_far, "gy", far_pairs(sizes[1]))
        y_near = lax.ppermute(y_near, "gy", near_pairs(sizes[1]))
        x_far = lax.ppermute(x_far, "gx", turn_pairs(sizes[0]))
        x_near = lax.ppermute(x_near, "gx", near_pairs(sizes[0]))
        return [x_far, y_far, y_near, x_near]

    cols = jnp.transpose(block_cols, (0, 3, 1, 2))
    place, stored, begin, degree, own, marks, *outgoing = call(
        functools.partial(first_kernel, sizes),
        [
            shape(cells, 4 * edges, dtype=BF16),
            shape(blocks, 2 * block, slots * block, dtype=BF16),
            field,
            shape(8, cells),
            shape(8, LANES),
            shape(8, 4 * edges, dtype=jnp.int32),
        ]
        + sends,
        [SM, VM] + [HBM] * 3,
        scratch_shapes=[
            pltpu.VMEM((4, edges), jnp.int32),
            pltpu.VMEM((vecs, cells), F32),
            pltpu.VMEM((blocks, slots, block, block), F32),
            pltpu.VMEM((cells, LANES), BF16),
            pltpu.SemaphoreType.DMA((blocks + 2,)),
        ],
    )(
        cols,
        live_counts,
        *(pltpu.with_memory_space_constraint(x, pltpu.HBM) for x in (edge_rows, basis, block_vals)),
    )
    stages = [
        (axis, 1 << b) for axis, size in zip(("gx", "gy"), sizes) for b in range(size.bit_length() - 1)
    ]
    arrived = exchange(outgoing)
    peak = spread(own, jnp.maximum, stages)
    local, edge_local, same, back = call(
        open_kernel,
        [
            field,
            edge_field,
            shape(4 * edges, 4 * edges, dtype=BF16),
            shape(4 * edges, cells, dtype=BF16),
        ],
        [SM] + [VM] * 6,
        scratch_shapes=scratch,
    )(cols, live_counts, begin, stored, degree, place, marks)

    history, earlier = [outgoing], [begin, begin]
    for number in range(3):
        bound = peak if number else own
        before = [x for parts in history for x in parts] if number == 1 else []
        outgoing = call(
            lambda *refs, number=number, count=len(before): edges_kernel(
                number, *refs[:8], refs[8 : 8 + count], *refs[8 + count :]
            ),
            sends,
            [VM] * (8 + len(before)),
        )(*arrived, edge_local, same, own, bound, *before)
        history.append(outgoing)
        coming = exchange(outgoing)
        now, local, edge_local, *base = call(
            functools.partial(field_kernel, number),
            [field, field, edge_field] + [shape(vecs, vecs)] * (number == 2),
            [SM] + [VM] * 14,
            scratch_shapes=scratch,
        )(cols, live_counts, *arrived, local, stored, degree, place, back, own, bound, *earlier)
        earlier = [begin, now] if number == 0 else [now, now]
        arrived = coming

    gram = call(gram_kernel, shape(vecs // 2, LANES), [VM] * 8)(*arrived, edge_local, same, peak, *base)
    gram = spread(gram, jnp.add, stages[:1])
    if sizes == (8, 4):
        parts = all_of(total(all_of(gram, "gx", (4, 6, 2))), "gy", (3, 2, 1))
    else:
        parts = [spread(gram, jnp.add, stages[1:])]
    now = call(last_kernel, shape(3 * vecs, cells, dtype=BF16), [VM] * 7)(*arrived, local, back, peak)
    root = math.sqrt(cells * sizes[0] * sizes[1])
    return call(functools.partial(encode_kernel, root), shape(1, 1, vecs, cells), [VM] * (len(parts) + 1))(
        *parts, now
    )


def solution(mesh):
    in_specs = (
        P("gx", "gy", None, None),
        P("gx", "gy", None, None, None, None),
        P("gx", "gy", None, None),
        P("gx", "gy", None, None),
        P("gx", "gy"),
    )
    out_specs = P("gx", "gy", None, None)

    return jax.shard_map(per_device, mesh=mesh, in_specs=in_specs, out_specs=out_specs, check_vma=False)
```

```python
import functools
import math

import jax
import jax.numpy as jnp
from jax import lax
from jax.experimental import pallas as pl
from jax.experimental.pallas import tpu as pltpu
from jax.sharding import PartitionSpec as P


LOWER_FRACTION = 0.125
LANES = 128
SHIFT = 7
CHUNK = 256
F32 = jnp.float32
BF16 = jnp.bfloat16
NT = (((1,), (1,)), ((), ()))
VM = pl.BlockSpec(memory_space=pltpu.VMEM)
SM = pl.BlockSpec(memory_space=pltpu.SMEM)
HBM = pl.BlockSpec(memory_space=pltpu.HBM)
LIMIT = 24 << 20
SIDES = (("gx", 1), ("gy", 1), ("gy", 0), ("gx", 0))


def split(x):
    hi = x.astype(BF16)
    return hi, (x - hi.astype(F32)).astype(BF16)


def stacked(x):
    return jnp.concatenate(split(x), axis=0)


def folded(x):
    half = x.shape[0] // 2
    return x[:half] + x[half:]


def dot(a, b):
    return jnp.dot(a, b, preferred_element_type=F32)


def dot_nt(a, b):
    return lax.dot_general(a, b, NT, preferred_element_type=F32)


def product_nt(a, b):
    left, right = stacked(a), stacked(b)
    product = folded(dot_nt(left, right))
    half = product.shape[1] // 2
    return product[:, :half] + product[:, half:]


def total(terms):
    terms = list(terms)
    while len(terms) > 1:
        terms = [a + b for a, b in zip(terms[::2], terms[1::2])] + terms[len(terms) & ~1 :]
    return terms[0]


def near_pairs(size):
    return [(i, i ^ 1) for i in range(size)]


def far_pairs(size):
    return [(i, (i + 1 if i % 2 else i - 1) % size) for i in range(size)]


def turn_pairs(size):
    up = [(i, i + 2 if i + 2 < size else i + 1) for i in range(0, size, 2)]
    down = [(i, i - 2 if i > 1 else 0) for i in range(1, size, 2)]
    return up + down


def xor_pairs(size, bit):
    return [(i, i ^ bit) for i in range(size)]


def live_lanes(count, start, width):
    return lax.broadcasted_iota(jnp.int32, (1, width), 1) + start < count


def left_rows(value):
    hi, lo = split(value)
    return jnp.concatenate(
        [
            jnp.concatenate([hi, hi], axis=1),
            jnp.concatenate([lo, jnp.zeros_like(lo)], axis=1),
        ],
        axis=0,
    )


def scalars(peak):
    upper = 2.0 * peak[0:1, 0:1]
    lower = LOWER_FRACTION * upper
    return (upper + lower) / 2.0, (upper - lower) / 2.0


def first_kernel(sizes, counts, cols_any, lists_any, basis_any, weights_any, *refs):
    place, stored, begin, degree, peak, marks = refs[:6]
    outs = refs[6:10]
    lists, basis, weights, hits, cols, sems = refs[10:]
    blocks, slots = weights.shape[:2]
    cells, edges = place.shape
    width = edges // len(outs)
    loads = [
        pltpu.make_async_copy(lists_any.at[0, 0], lists, sems.at[blocks]),
        pltpu.make_async_copy(basis_any.at[0, 0], basis, sems.at[blocks + 1]),
        pltpu.make_async_copy(cols_any, cols, sems.at[blocks + 2]),
    ]
    blocks_in = [
        pltpu.make_async_copy(weights_any.at[0, 0, m], weights.at[m], sems.at[m]) for m in range(blocks)
    ]
    for load in loads:
        load.start()
    count = counts[...]
    degree[...] = jnp.zeros_like(degree)
    loads[0].wait()
    for load in blocks_in:
        load.start()
    loads[1].wait()
    order = []
    for axis, shift in SIDES:
        dim = ("gx", "gy").index(axis)
        me = lax.axis_index(axis)
        upward = me % 2 == shift
        low, high = lists[2 * dim : 2 * dim + 1], lists[2 * dim + 1 : 2 * dim + 2]
        low, high = jnp.where(me > 0, low, -1), jnp.where(me < sizes[dim] - 1, high, -1)
        order.append(jnp.where(upward, high, low))
    targets = jnp.concatenate(order, axis=1)
    marks[...] = jnp.broadcast_to(targets, marks.shape)
    spot = lax.broadcasted_iota(jnp.int32, (LANES, edges), 0)
    within = (spot == (targets & (LANES - 1))).astype(F32).astype(BF16)
    block = jnp.broadcast_to((targets >> SHIFT).astype(F32).astype(BF16), within.shape)
    for m in range(blocks):
        equal = jnp.where(block == BF16(m), within, jnp.zeros_like(within))
        place[m * LANES : (m + 1) * LANES] = equal
        hits[m * LANES : (m + 1) * LANES] = total(
            equal[:, other : other + LANES] for other in range(0, edges, LANES)
        )
    begin[...] = jnp.where(live_lanes(count, 0, cells), basis[...], 0.0)
    picked = folded(dot(stacked(begin[...]), place[...]))
    for i, out in enumerate(outs):
        out[...] = picked[:, i * width : (i + 1) * width]
    joined = dot_nt(jnp.ones((16, LANES), BF16), hits[...])[:8]
    rows = lax.broadcasted_iota(jnp.int32, (LANES, LANES), 0)
    loads[2].wait()
    for m in range(blocks):
        blocks_in[m].wait()
        live = rows + m * LANES < count
        for j in range(slots):
            value = weights[m, j]
            hi, lo = split(value)
            stored[m, 0:LANES, j * LANES : (j + 1) * LANES] = hi
            stored[m, LANES : 2 * LANES, j * LANES : (j + 1) * LANES] = lo
            kept = jnp.where(live, value, 0.0)
            spot = pl.ds(pl.multiple_of(cols[0, j, 0, m] * LANES, LANES), LANES)
            degree[:, spot] += total(kept[i : i + 8] for i in range(0, LANES, 8))
    value = jnp.sum(degree[...], axis=0, keepdims=True) + joined
    value = jnp.where(live_lanes(count, 0, cells), value, 0.0)
    degree[...] = value
    peak[...] = jnp.full(peak.shape, jnp.max(value), F32)


def multiply(cols, values, stored, inside):
    blocks, _, width = stored.shape
    inside[...] = jnp.zeros_like(inside)
    for m in range(blocks):
        product = folded(dot(left_rows(values[:, m * LANES : (m + 1) * LANES]), stored[m]))
        for j in range(width // LANES):
            spot = pl.ds(pl.multiple_of(cols[0, j, 0, m] * LANES, LANES), LANES)
            inside[:, spot] += product[:, j * LANES : (j + 1) * LANES]


def gather(values, place):
    return folded(dot(stacked(values), place[...]))


def joined_up(parts, vecs):
    return jnp.concatenate([part[:vecs] for part in parts], axis=1)


def chunks(cells):
    return [slice(start, start + CHUNK) for start in range(0, cells, CHUNK)]


def open_kernel(cols, counts, begin, stored, degree, place, marks, local, edge_local, same, back, inside):
    cells, edges = place.shape
    targets = marks[0:1]
    for start in range(0, edges, LANES):
        across = jnp.broadcast_to(targets[:, start : start + LANES], (LANES, LANES))
        down = across.astype(F32).T.astype(jnp.int32)
        down = jnp.where(down < 0, -2, down)
        for other in range(0, edges, LANES):
            equal = down == targets[:, other : other + LANES]
            same[start : start + LANES, other : other + LANES] = equal.astype(F32).astype(BF16)
        lane = lax.broadcasted_iota(jnp.int32, (LANES, LANES), 1)
        within = ((down & (LANES - 1)) == lane).astype(F32).astype(BF16)
        block = (down >> SHIFT).astype(F32).astype(BF16)
        for m in range(cells // LANES):
            equal = jnp.where(block == BF16(m), within, jnp.zeros_like(within))
            back[start : start + LANES, m * LANES : (m + 1) * LANES] = equal
    multiply(cols, begin, stored, inside)
    for part in chunks(cells):
        live = live_lanes(counts[...], part.start, CHUNK)
        local[:, part] = degree[0:1, part] * begin[:, part] - jnp.where(live, inside[:, part], 0.0)
    edge_local[...] = gather(local[...], place)


def edges_kernel(number, r0, r1, r2, r3, edge_local, same, own, peak, before, *outs):
    vecs = edge_local.shape[0]
    crossed = folded(dot(stacked(joined_up((r0, r1, r2, r3), vecs)), same[...]))
    if number == 0:
        value = edge_local[...] - crossed
    elif number == 1:
        centre, half = scalars(peak)
        top = own[0:1, 0:1]
        first, second = joined_up(before[:4], vecs), joined_up(before[4:], vecs)
        value = second_field(centre, half, top, edge_local[...] - crossed / top, second, first)[1]
    else:
        _, half = scalars(peak)
        value = edge_local[...] - (2.0 / half) * crossed
    width = value.shape[1] // len(outs)
    for i, out in enumerate(outs):
        out[:vecs] = value[:, i * width : (i + 1) * width]
        if out.shape[0] > vecs:
            out[vecs:] = jnp.broadcast_to(peak[0:1, 0:1], (out.shape[0] - vecs, width))


def second_field(centre, half, top, twice, once, begin):
    ratio = centre / half
    shrunk = once / half
    first = shrunk - ratio * begin
    second = (2.0 / half) * (top / half) * twice - 2.0 * ratio * (shrunk + first) - begin
    return first, second


def field_kernel(
    number, cols, counts, r0, r1, r2, r3, local, stored, degree, place, back, own, peak, begin, once, *refs
):
    field, later, edge_local = refs[:3]
    inside = refs[-1]
    cells = place.shape[0]
    top = own[0:1, 0:1]
    centre, half = scalars(peak)
    arrived = stacked(joined_up((r0, r1, r2, r3), local.shape[0]))
    for part in chunks(cells):
        crossed = folded(dot(arrived, back[:, part]))
        if number == 0:
            value = (local[:, part] - crossed) / top
        elif number == 1:
            first, value = second_field(
                centre, half, top, local[:, part] - crossed / top, once[:, part] * top, begin[:, part]
            )
            later[:, part] = first
        else:
            value = local[:, part] - (2.0 / half) * crossed
            later[:, part] = begin[:, part]
        field[:, part] = value
    multiply(cols, field, stored, inside)
    for part in chunks(cells):
        live = live_lanes(counts[...], part.start, CHUNK)
        kept = jnp.where(live, inside[:, part], 0.0)
        if number == 0:
            later[:, part] = degree[0:1, part] * field[:, part] - kept
        else:
            value = (degree[0:1, part] - centre) * field[:, part] - kept
            later[:, part] = (2.0 / half) * value - later[:, part]
    edge_local[...] = gather(later[...], place)
    if number == 2:
        refs[3][...] = product_nt(later[...], later[...])


def places(size):
    row = lax.broadcasted_iota(jnp.int32, (size, size), 0)
    return row, lax.broadcasted_iota(jnp.int32, (size, size), 1)


def packed(gram):
    size = gram.shape[0] // 2
    row, col = places(size)
    low, high = gram[:size, :size], gram[size:, size:]
    diagonal = jnp.sum(jnp.where(row == col, high, 0.0), axis=1, keepdims=True)
    width = LANES - 2 * size
    return jnp.concatenate(
        [jnp.where(col <= row, low, high), gram[:size, size:], jnp.broadcast_to(diagonal, (size, width))],
        axis=1,
    )


def unpacked(value):
    size = value.shape[0]
    row, col = places(size)
    mixed, cross = value[:, :size], value[:, size : 2 * size]
    below, above = jnp.where(col < row, mixed, 0.0), jnp.where(col > row, mixed, 0.0)
    diagonal = jnp.where(row == col, value[:, 2 * size : 2 * size + 1], 0.0)
    low = jnp.where(row == col, mixed, below) + below.T
    high = above + above.T + diagonal
    return jnp.concatenate(
        [jnp.concatenate([low, cross], axis=1), jnp.concatenate([cross.T, high], axis=1)], axis=0
    )


def gram_kernel(r0, r1, r2, r3, edge_local, same, peak, base, gram):
    _, half = scalars(peak)
    scale = 2.0 / half
    arrived = joined_up((r0, r1, r2, r3), edge_local.shape[0])
    crossed = folded(dot(stacked(arrived), same[...]))
    mixed = product_nt(scale * (edge_local[...] - (0.5 * scale) * crossed), arrived)
    gram[...] = packed(base[...] - mixed - mixed.T)


def last_kernel(r0, r1, r2, r3, local, back, peak, terms):
    _, half = scalars(peak)
    arrived = stacked(joined_up((r0, r1, r2, r3), local.shape[0]))
    for part in chunks(back.shape[1]):
        hi, lo = split(local[:, part] - (2.0 / half) * folded(dot(arrived, back[:, part])))
        terms[:, part] = jnp.concatenate([hi, lo, hi], axis=0)


def eliminate(block, start, right):
    size, width = block.shape
    near = [
        [jnp.broadcast_to(block[i : i + 1, start + j : start + j + 1], (size, width)) for j in range(i + 1)]
        for i in range(size)
    ]
    rows, factors, inverses = list(right), [[] for _ in range(size)], []
    for k in range(size):
        inverses.append(1.0 / near[k][k])
        for i in range(k + 1, size):
            factor = near[i][k] * inverses[k]
            factors[i].append(factor)
            for j in range(k + 1, i + 1):
                near[i][j] = near[i][j] - factor * near[j][k]
            rows[i] = rows[i] - factor * rows[k]
    half = [lax.rsqrt(near[i][i]) * rows[i] for i in range(size)]
    whole = [rows[i] * inverses[i] for i in range(size)]
    for i in reversed(range(size)):
        for j in range(i):
            whole[j] = whole[j] - factors[i][j] * whole[i]
    return half, whole


def encode_kernel(root, *refs):
    *parts, values, out = refs
    gram = unpacked(total(part[...] for part in parts))
    vecs = gram.shape[0]
    size = 8
    lane = lax.broadcasted_iota(jnp.int32, (size, vecs), 1)
    sub = lax.broadcasted_iota(jnp.int32, (size, vecs), 0)
    rows = [gram[i * size : (i + 1) * size] for i in range(vecs // size)]
    for g in range(vecs // size):
        start = g * size
        inside = jnp.logical_and(lane >= start, lane < start + size)
        unit = jnp.where(inside, (lane - start == sub).astype(F32), rows[g])
        spread_rows = [jnp.broadcast_to(unit[j : j + 1], (size, vecs)) for j in range(size)]
        half, whole = eliminate(rows[g], start, spread_rows)
        for i in range(g + 1, vecs // size):
            kept = jnp.where(inside, 0.0, rows[i])
            rows[i] = kept - total(
                jnp.broadcast_to(rows[i][:, start + j : start + j + 1], (size, vecs)) * whole[j]
                for j in range(size)
            )
        done = half[0]
        for j in range(1, size):
            done = jnp.where(sub == j, half[j], done)
        rows[g] = jnp.where(lane < start + size, done, 0.0)
    hi, lo = split(jnp.concatenate(rows, axis=0) * root)
    out[0, 0] = dot(jnp.concatenate([hi, hi, lo], axis=1), values[...])


def call(kernel, shapes, specs, **extra):
    many = isinstance(shapes, (tuple, list))
    return pl.pallas_call(
        kernel,
        out_shape=shapes,
        in_specs=specs,
        out_specs=[VM] * len(shapes) if many else VM,
        compiler_params=pltpu.CompilerParams(vmem_limit_bytes=LIMIT),
        **extra,
    )


def shape(*dims, dtype=F32):
    return jax.ShapeDtypeStruct(dims, dtype)


def spread(value, combine, stages):
    for axis, bit in stages:
        pairs = xor_pairs(lax.axis_size(axis), bit)
        value = combine(value, lax.ppermute(value, axis, pairs))
    return value


def all_of(value, axis, bits):
    size = lax.axis_size(axis)
    return [value] + [lax.ppermute(value, axis, xor_pairs(size, bit)) for bit in bits]


def per_device(basis, block_vals, block_cols, edge_rows, live_counts):
    vecs, cells = basis.shape[2:]
    blocks, slots, block = block_vals.shape[2:5]
    edges = edge_rows.shape[3]
    sizes = (lax.axis_size("gx"), lax.axis_size("gy"))
    field = shape(vecs, cells)
    sends = [shape(vecs, edges)] * 4
    edge_field = shape(vecs, 4 * edges)
    scratch = [pltpu.VMEM((vecs, cells), F32)]

    def exchange(parts):
        x_far, y_far, y_near, x_near = parts
        x_far = lax.ppermute(x_far, "gx", near_pairs(sizes[0]))
        y_far = lax.ppermute(y_far, "gy", far_pairs(sizes[1]))
        y_near = lax.ppermute(y_near, "gy", near_pairs(sizes[1]))
        x_far = lax.ppermute(x_far, "gx", turn_pairs(sizes[0]))
        x_near = lax.ppermute(x_near, "gx", near_pairs(sizes[0]))
        return [x_far, y_far, y_near, x_near]

    cols = jnp.transpose(block_cols, (0, 3, 1, 2))
    place, stored, begin, degree, own, marks, *outgoing = call(
        functools.partial(first_kernel, sizes),
        [
            shape(cells, 4 * edges, dtype=BF16),
            shape(blocks, 2 * block, slots * block, dtype=BF16),
            field,
            shape(8, cells),
            shape(8, LANES),
            shape(8, 4 * edges, dtype=jnp.int32),
        ]
        + sends,
        [VM] + [HBM] * 4,
        scratch_shapes=[
            pltpu.VMEM((4, edges), jnp.int32),
            pltpu.VMEM((vecs, cells), F32),
            pltpu.VMEM((blocks, slots, block, block), F32),
            pltpu.VMEM((cells, LANES), BF16),
            pltpu.SMEM(cols.shape, jnp.int32),
            pltpu.SemaphoreType.DMA((blocks + 3,)),
        ],
    )(
        live_counts,
        *(pltpu.with_memory_space_constraint(x, pltpu.HBM) for x in (cols, edge_rows, basis, block_vals)),
    )
    stages = [
        (axis, 1 << b) for axis, size in zip(("gx", "gy"), sizes) for b in range(size.bit_length() - 1)
    ]
    arrived = exchange(outgoing)
    riding = sizes[1] == 4
    across = [stage for stage in stages if not (riding and stage[0] == "gy")]
    peak = spread(own, jnp.maximum, across)
    if riding:
        opposite = lax.ppermute(peak, "gy", xor_pairs(4, 2))
    local, edge_local, same, back = call(
        open_kernel,
        [
            field,
            edge_field,
            shape(4 * edges, 4 * edges, dtype=BF16),
            shape(4 * edges, cells, dtype=BF16),
        ],
        [SM] + [VM] * 6,
        scratch_shapes=scratch,
    )(cols, live_counts, begin, stored, degree, place, marks)

    history, earlier = [outgoing], [begin, begin]
    for number in range(3):
        wide = riding and number == 0
        if riding and number == 1:
            ridden = [part[vecs:, :LANES] for part, (axis, _) in zip(arrived, SIDES) if axis == "gy"]
            peak = jnp.maximum(jnp.maximum(peak, opposite), jnp.maximum(*ridden))
        bound = peak if number or riding else own
        before = [x for parts in history for x in parts] if number == 1 else []
        outgoing = call(
            lambda *refs, number=number, count=len(before): edges_kernel(
                number, *refs[:8], refs[8 : 8 + count], *refs[8 + count :]
            ),
            [shape(vecs + 8 * (wide and axis == "gy"), edges) for axis, _ in SIDES],
            [VM] * (8 + len(before)),
        )(*arrived, edge_local, same, own, bound, *before)
        history.append(outgoing)
        coming = exchange(outgoing)
        now, local, edge_local, *base = call(
            functools.partial(field_kernel, number),
            [field, field, edge_field] + [shape(vecs, vecs)] * (number == 2),
            [SM] + [VM] * 14,
            scratch_shapes=scratch,
        )(cols, live_counts, *arrived, local, stored, degree, place, back, own, bound if number else own, *earlier)
        earlier = [begin, now] if number == 0 else [now, now]
        arrived = coming

    gram = call(gram_kernel, shape(vecs // 2, LANES), [VM] * 8)(*arrived, edge_local, same, peak, *base)
    gram = spread(gram, jnp.add, stages[:1])
    if sizes == (8, 4):
        parts = all_of(total(all_of(gram, "gx", (4, 6, 2))), "gy", (3, 2, 1))
    else:
        parts = [spread(gram, jnp.add, stages[1:])]
    now = call(last_kernel, shape(3 * vecs, cells, dtype=BF16), [VM] * 7)(*arrived, local, back, peak)
    root = math.sqrt(cells * sizes[0] * sizes[1])
    return call(functools.partial(encode_kernel, root), shape(1, 1, vecs, cells), [VM] * (len(parts) + 1))(
        *parts, now
    )


def solution(mesh):
    in_specs = (
        P("gx", "gy", None, None),
        P("gx", "gy", None, None, None, None),
        P("gx", "gy", None, None),
        P("gx", "gy", None, None),
        P("gx", "gy"),
    )
    out_specs = P("gx", "gy", None, None)

    return jax.shard_map(per_device, mesh=mesh, in_specs=in_specs, out_specs=out_specs, check_vma=False)
```

```python
import functools
import math

import jax
import jax.numpy as jnp
from jax import lax
from jax.experimental import pallas as pl
from jax.experimental.pallas import tpu as pltpu
from jax.sharding import PartitionSpec as P


LOWER_FRACTION = 0.125
LANES = 128
SHIFT = 7
CHUNK = 256
F32 = jnp.float32
BF16 = jnp.bfloat16
NT = (((1,), (1,)), ((), ()))
VM = pl.BlockSpec(memory_space=pltpu.VMEM)
SM = pl.BlockSpec(memory_space=pltpu.SMEM)
HBM = pl.BlockSpec(memory_space=pltpu.HBM)
LIMIT = 24 << 20
SIDES = (("gx", 1), ("gy", 1), ("gy", 0), ("gx", 0))


def split(x):
    hi = x.astype(BF16)
    return hi, (x - hi.astype(F32)).astype(BF16)


def stacked(x):
    return jnp.concatenate(split(x), axis=0)


def folded(x):
    half = x.shape[0] // 2
    return x[:half] + x[half:]


def dot(a, b):
    return jnp.dot(a, b, preferred_element_type=F32)


def dot_nt(a, b):
    return lax.dot_general(a, b, NT, preferred_element_type=F32)


def product_nt(a, b):
    left, right = stacked(a), stacked(b)
    product = folded(dot_nt(left, right))
    half = product.shape[1] // 2
    return product[:, :half] + product[:, half:]


def total(terms):
    terms = list(terms)
    while len(terms) > 1:
        terms = [a + b for a, b in zip(terms[::2], terms[1::2])] + terms[len(terms) & ~1 :]
    return terms[0]


def near_pairs(size):
    return [(i, i ^ 1) for i in range(size)]


def far_pairs(size):
    return [(i, (i + 1 if i % 2 else i - 1) % size) for i in range(size)]


def turn_pairs(size):
    up = [(i, i + 2 if i + 2 < size else i + 1) for i in range(0, size, 2)]
    down = [(i, i - 2 if i > 1 else 0) for i in range(1, size, 2)]
    return up + down


def xor_pairs(size, bit):
    return [(i, i ^ bit) for i in range(size)]


def live_lanes(count, start, width):
    return lax.broadcasted_iota(jnp.int32, (1, width), 1) + start < count


def left_rows(value):
    hi, lo = split(value)
    return jnp.concatenate(
        [
            jnp.concatenate([hi, hi], axis=1),
            jnp.concatenate([lo, jnp.zeros_like(lo)], axis=1),
        ],
        axis=0,
    )


def scalars(peak):
    upper = 2.0 * peak[0:1, 0:1]
    lower = LOWER_FRACTION * upper
    return (upper + lower) / 2.0, (upper - lower) / 2.0


def first_kernel(sizes, counts, cols_any, lists_any, basis_any, weights_any, *refs):
    place, stored, begin, degree, peak, marks = refs[:6]
    outs = refs[6:10]
    lists, basis, weights, hits, cols, sems = refs[10:]
    blocks, slots = weights.shape[:2]
    cells, edges = place.shape
    width = edges // len(outs)
    loads = [
        pltpu.make_async_copy(lists_any.at[0, 0], lists, sems.at[blocks]),
        pltpu.make_async_copy(basis_any.at[0, 0], basis, sems.at[blocks + 1]),
        pltpu.make_async_copy(cols_any, cols, sems.at[blocks + 2]),
    ]
    blocks_in = [
        pltpu.make_async_copy(weights_any.at[0, 0, m], weights.at[m], sems.at[m]) for m in range(blocks)
    ]
    for load in loads:
        load.start()
    count = counts[...]
    degree[...] = jnp.zeros_like(degree)
    loads[0].wait()
    for load in blocks_in:
        load.start()
    loads[1].wait()
    order = []
    for axis, shift in SIDES:
        dim = ("gx", "gy").index(axis)
        me = lax.axis_index(axis)
        upward = me % 2 == shift
        low, high = lists[2 * dim : 2 * dim + 1], lists[2 * dim + 1 : 2 * dim + 2]
        low, high = jnp.where(me > 0, low, -1), jnp.where(me < sizes[dim] - 1, high, -1)
        order.append(jnp.where(upward, high, low))
    targets = jnp.concatenate(order, axis=1)
    marks[...] = jnp.broadcast_to(targets, marks.shape)
    spot = lax.broadcasted_iota(jnp.int32, (LANES, edges), 0)
    within = (spot == (targets & (LANES - 1))).astype(F32).astype(BF16)
    block = jnp.broadcast_to((targets >> SHIFT).astype(F32).astype(BF16), within.shape)
    for m in range(blocks):
        equal = jnp.where(block == BF16(m), within, jnp.zeros_like(within))
        place[m * LANES : (m + 1) * LANES] = equal
        hits[m * LANES : (m + 1) * LANES] = total(
            equal[:, other : other + LANES] for other in range(0, edges, LANES)
        )
    begin[...] = jnp.where(live_lanes(count, 0, cells), basis[...], 0.0)
    picked = folded(dot(stacked(begin[...]), place[...]))
    for i, out in enumerate(outs):
        out[...] = picked[:, i * width : (i + 1) * width]
    joined = dot_nt(jnp.ones((16, LANES), BF16), hits[...])[:8]
    rows = lax.broadcasted_iota(jnp.int32, (LANES, LANES), 0)
    loads[2].wait()
    for m in range(blocks):
        blocks_in[m].wait()
        live = rows + m * LANES < count
        for j in range(slots):
            value = weights[m, j]
            hi, lo = split(value)
            stored[m, 0:LANES, j * LANES : (j + 1) * LANES] = hi
            stored[m, LANES : 2 * LANES, j * LANES : (j + 1) * LANES] = lo
            kept = jnp.where(live, value, 0.0)
            spot = pl.ds(pl.multiple_of(cols[0, j, 0, m] * LANES, LANES), LANES)
            degree[:, spot] += total(kept[i : i + 8] for i in range(0, LANES, 8))
    value = jnp.sum(degree[...], axis=0, keepdims=True) + joined
    value = jnp.where(live_lanes(count, 0, cells), value, 0.0)
    degree[...] = value
    peak[...] = jnp.full(peak.shape, jnp.max(value), F32)


def multiply(cols, values, stored, inside):
    blocks, _, width = stored.shape
    inside[...] = jnp.zeros_like(inside)
    for m in range(blocks):
        product = folded(dot(left_rows(values[:, m * LANES : (m + 1) * LANES]), stored[m]))
        for j in range(width // LANES):
            spot = pl.ds(pl.multiple_of(cols[0, j, 0, m] * LANES, LANES), LANES)
            inside[:, spot] += product[:, j * LANES : (j + 1) * LANES]


def gather(values, place):
    return folded(dot(stacked(values), place[...]))


def joined_up(parts, vecs):
    return jnp.concatenate([part[:vecs] for part in parts], axis=1)


def chunks(cells):
    return [slice(start, start + CHUNK) for start in range(0, cells, CHUNK)]


def open_kernel(cols, counts, begin, stored, degree, place, marks, local, edge_local, same, back, inside):
    cells, edges = place.shape
    targets = marks[0:1]
    for start in range(0, edges, LANES):
        across = jnp.broadcast_to(targets[:, start : start + LANES], (LANES, LANES))
        down = across.astype(F32).T.astype(jnp.int32)
        down = jnp.where(down < 0, -2, down)
        for other in range(0, edges, LANES):
            equal = down == targets[:, other : other + LANES]
            same[start : start + LANES, other : other + LANES] = equal.astype(F32).astype(BF16)
        lane = lax.broadcasted_iota(jnp.int32, (LANES, LANES), 1)
        within = ((down & (LANES - 1)) == lane).astype(F32).astype(BF16)
        block = (down >> SHIFT).astype(F32).astype(BF16)
        for m in range(cells // LANES):
            equal = jnp.where(block == BF16(m), within, jnp.zeros_like(within))
            back[start : start + LANES, m * LANES : (m + 1) * LANES] = equal
    multiply(cols, begin, stored, inside)
    for part in chunks(cells):
        live = live_lanes(counts[...], part.start, CHUNK)
        local[:, part] = degree[0:1, part] * begin[:, part] - jnp.where(live, inside[:, part], 0.0)
    edge_local[...] = gather(local[...], place)


def edges_kernel(number, r0, r1, r2, r3, edge_local, same, own, peak, before, *outs):
    vecs = edge_local.shape[0]
    crossed = folded(dot(stacked(joined_up((r0, r1, r2, r3), vecs)), same[...]))
    if number == 0:
        value = edge_local[...] - crossed
    elif number == 1:
        centre, half = scalars(peak)
        top = own[0:1, 0:1]
        first, second = joined_up(before[:4], vecs), joined_up(before[4:], vecs)
        value = second_field(centre, half, top, edge_local[...] - crossed / top, second, first)[1]
    else:
        _, half = scalars(peak)
        value = edge_local[...] - (2.0 / half) * crossed
    width = value.shape[1] // len(outs)
    for i, out in enumerate(outs):
        out[:vecs] = value[:, i * width : (i + 1) * width]
        if out.shape[0] > vecs:
            out[vecs:] = jnp.broadcast_to(peak[0:1, 0:1], (out.shape[0] - vecs, width))


def second_field(centre, half, top, twice, once, begin):
    ratio = centre / half
    shrunk = once / half
    first = shrunk - ratio * begin
    second = (2.0 / half) * (top / half) * twice - 2.0 * ratio * (shrunk + first) - begin
    return first, second


def field_kernel(
    number, cols, counts, r0, r1, r2, r3, local, stored, degree, place, back, own, peak, begin, once, *refs
):
    field, later, edge_local = refs[:3]
    inside = refs[-1]
    cells = place.shape[0]
    top = own[0:1, 0:1]
    centre, half = scalars(peak)
    arrived = stacked(joined_up((r0, r1, r2, r3), local.shape[0]))
    for part in chunks(cells):
        crossed = folded(dot(arrived, back[:, part]))
        if number == 0:
            value = (local[:, part] - crossed) / top
        elif number == 1:
            first, value = second_field(
                centre, half, top, local[:, part] - crossed / top, once[:, part] * top, begin[:, part]
            )
            later[:, part] = first
        else:
            value = local[:, part] - (2.0 / half) * crossed
        field[:, part] = value
    multiply(cols, field, stored, inside)
    for part in chunks(cells):
        live = live_lanes(counts[...], part.start, CHUNK)
        kept = jnp.where(live, inside[:, part], 0.0)
        if number == 0:
            later[:, part] = degree[0:1, part] * field[:, part] - kept
        else:
            value = (degree[0:1, part] - centre) * field[:, part] - kept
            before = later[:, part] if number == 1 else begin[:, part]
            later[:, part] = (2.0 / half) * value - before
    edge_local[...] = gather(later[...], place)
    if number == 2:
        refs[3][...] = product_nt(later[...], later[...])


def places(size):
    row = lax.broadcasted_iota(jnp.int32, (size, size), 0)
    return row, lax.broadcasted_iota(jnp.int32, (size, size), 1)


def packed(gram):
    size = gram.shape[0] // 2
    row, col = places(size)
    low, high = gram[:size, :size], gram[size:, size:]
    diagonal = jnp.sum(jnp.where(row == col, high, 0.0), axis=1, keepdims=True)
    width = LANES - 2 * size
    return jnp.concatenate(
        [jnp.where(col <= row, low, high), gram[:size, size:], jnp.broadcast_to(diagonal, (size, width))],
        axis=1,
    )


def unpacked(value):
    size = value.shape[0]
    row, col = places(size)
    mixed, cross = value[:, :size], value[:, size : 2 * size]
    below, above = jnp.where(col < row, mixed, 0.0), jnp.where(col > row, mixed, 0.0)
    diagonal = jnp.where(row == col, value[:, 2 * size : 2 * size + 1], 0.0)
    low = jnp.where(row == col, mixed, below) + below.T
    high = above + above.T + diagonal
    return jnp.concatenate(
        [jnp.concatenate([low, cross], axis=1), jnp.concatenate([cross.T, high], axis=1)], axis=0
    )


def gram_kernel(r0, r1, r2, r3, edge_local, same, peak, base, gram):
    _, half = scalars(peak)
    scale = 2.0 / half
    arrived = joined_up((r0, r1, r2, r3), edge_local.shape[0])
    crossed = folded(dot(stacked(arrived), same[...]))
    mixed = product_nt(scale * (edge_local[...] - (0.5 * scale) * crossed), arrived)
    gram[...] = packed(base[...] - mixed - mixed.T)


def last_kernel(r0, r1, r2, r3, local, back, peak, terms):
    _, half = scalars(peak)
    arrived = stacked(joined_up((r0, r1, r2, r3), local.shape[0]))
    for part in chunks(back.shape[1]):
        hi, lo = split(local[:, part] - (2.0 / half) * folded(dot(arrived, back[:, part])))
        terms[:, part] = jnp.concatenate([hi, lo, hi], axis=0)


def eliminate(block, start, right, tiles):
    size, width = block.shape
    for j in range(size):
        tiles[j] = jnp.broadcast_to(block[:, start + j : start + j + 1], (size, width))
    near = [
        [jnp.broadcast_to(tiles[j, i : i + 1], (size, width)) for j in range(i + 1)] for i in range(size)
    ]
    rows, factors, inverses = list(right), [[] for _ in range(size)], []
    for k in range(size):
        inverses.append(1.0 / near[k][k])
        for i in range(k + 1, size):
            factor = near[i][k] * inverses[k]
            factors[i].append(factor)
            for j in range(k + 1, i + 1):
                near[i][j] = near[i][j] - factor * near[j][k]
            rows[i] = rows[i] - factor * rows[k]
    half = [lax.rsqrt(near[i][i]) * rows[i] for i in range(size)]
    whole = [rows[i] * inverses[i] for i in range(size)]
    for i in reversed(range(size)):
        for j in range(i):
            whole[j] = whole[j] - factors[i][j] * whole[i]
    return half, whole


def encode_kernel(root, *refs):
    *parts, values, out, tiles = refs
    gram = unpacked(total(part[...] for part in parts))
    vecs = gram.shape[0]
    size = 8
    lane = lax.broadcasted_iota(jnp.int32, (size, vecs), 1)
    sub = lax.broadcasted_iota(jnp.int32, (size, vecs), 0)
    rows = [gram[i * size : (i + 1) * size] for i in range(vecs // size)]
    for g in range(vecs // size):
        start = g * size
        inside = jnp.logical_and(lane >= start, lane < start + size)
        unit = jnp.where(inside, (lane - start == sub).astype(F32), rows[g])
        spread_rows = [jnp.broadcast_to(unit[j : j + 1], (size, vecs)) for j in range(size)]
        half, whole = eliminate(rows[g], start, spread_rows, tiles.at[g % 2])
        for i in range(g + 1, vecs // size):
            kept = jnp.where(inside, 0.0, rows[i])
            rows[i] = kept - total(
                jnp.broadcast_to(rows[i][:, start + j : start + j + 1], (size, vecs)) * whole[j]
                for j in range(size)
            )
        done = half[0]
        for j in range(1, size):
            done = jnp.where(sub == j, half[j], done)
        rows[g] = jnp.where(lane < start + size, done, 0.0)
    hi, lo = split(jnp.concatenate(rows, axis=0) * root)
    out[0, 0] = dot(jnp.concatenate([hi, hi, lo], axis=1), values[...])


def call(kernel, shapes, specs, **extra):
    many = isinstance(shapes, (tuple, list))
    return pl.pallas_call(
        kernel,
        out_shape=shapes,
        in_specs=specs,
        out_specs=[VM] * len(shapes) if many else VM,
        compiler_params=pltpu.CompilerParams(vmem_limit_bytes=LIMIT),
        **extra,
    )


def shape(*dims, dtype=F32):
    return jax.ShapeDtypeStruct(dims, dtype)


def spread(value, combine, stages):
    for axis, bit in stages:
        pairs = xor_pairs(lax.axis_size(axis), bit)
        value = combine(value, lax.ppermute(value, axis, pairs))
    return value


def all_of(value, axis, bits):
    size = lax.axis_size(axis)
    return [value] + [lax.ppermute(value, axis, xor_pairs(size, bit)) for bit in bits]


def per_device(basis, block_vals, block_cols, edge_rows, live_counts):
    vecs, cells = basis.shape[2:]
    blocks, slots, block = block_vals.shape[2:5]
    edges = edge_rows.shape[3]
    sizes = (lax.axis_size("gx"), lax.axis_size("gy"))
    field = shape(vecs, cells)
    sends = [shape(vecs, edges)] * 4
    edge_field = shape(vecs, 4 * edges)
    scratch = [pltpu.VMEM((vecs, cells), F32)]

    def exchange(parts):
        x_far, y_far, y_near, x_near = parts
        x_far = lax.ppermute(x_far, "gx", near_pairs(sizes[0]))
        y_far = lax.ppermute(y_far, "gy", far_pairs(sizes[1]))
        y_near = lax.ppermute(y_near, "gy", near_pairs(sizes[1]))
        x_far = lax.ppermute(x_far, "gx", turn_pairs(sizes[0]))
        x_near = lax.ppermute(x_near, "gx", near_pairs(sizes[0]))
        return [x_far, y_far, y_near, x_near]

    cols = jnp.transpose(block_cols, (0, 3, 1, 2))
    place, stored, begin, degree, own, marks, *outgoing = call(
        functools.partial(first_kernel, sizes),
        [
            shape(cells, 4 * edges, dtype=BF16),
            shape(blocks, 2 * block, slots * block, dtype=BF16),
            field,
            shape(8, cells),
            shape(8, LANES),
            shape(8, 4 * edges, dtype=jnp.int32),
        ]
        + sends,
        [VM] + [HBM] * 4,
        scratch_shapes=[
            pltpu.VMEM((4, edges), jnp.int32),
            pltpu.VMEM((vecs, cells), F32),
            pltpu.VMEM((blocks, slots, block, block), F32),
            pltpu.VMEM((cells, LANES), BF16),
            pltpu.SMEM(cols.shape, jnp.int32),
            pltpu.SemaphoreType.DMA((blocks + 3,)),
        ],
    )(
        live_counts,
        *(pltpu.with_memory_space_constraint(x, pltpu.HBM) for x in (cols, edge_rows, basis, block_vals)),
    )
    stages = [
        (axis, 1 << b) for axis, size in zip(("gx", "gy"), sizes) for b in range(size.bit_length() - 1)
    ]
    arrived = exchange(outgoing)
    riding = sizes[1] == 4
    across = [stage for stage in stages if not (riding and stage[0] == "gy")]
    peak = spread(own, jnp.maximum, across)
    if riding:
        opposite = lax.ppermute(peak, "gy", xor_pairs(4, 2))
    local, edge_local, same, back = call(
        open_kernel,
        [
            field,
            edge_field,
            shape(4 * edges, 4 * edges, dtype=BF16),
            shape(4 * edges, cells, dtype=BF16),
        ],
        [SM] + [VM] * 6,
        scratch_shapes=scratch,
    )(cols, live_counts, begin, stored, degree, place, marks)

    history, earlier = [outgoing], [begin, begin]
    for number in range(3):
        wide = riding and number == 0
        if riding and number == 1:
            ridden = [part[vecs:, :LANES] for part, (axis, _) in zip(arrived, SIDES) if axis == "gy"]
            peak = jnp.maximum(jnp.maximum(peak, opposite), jnp.maximum(*ridden))
        bound = peak if number or riding else own
        before = [x for parts in history for x in parts] if number == 1 else []
        outgoing = call(
            lambda *refs, number=number, count=len(before): edges_kernel(
                number, *refs[:8], refs[8 : 8 + count], *refs[8 + count :]
            ),
            [shape(vecs + 8 * (wide and axis == "gy"), edges) for axis, _ in SIDES],
            [VM] * (8 + len(before)),
        )(*arrived, edge_local, same, own, bound, *before)
        history.append(outgoing)
        coming = exchange(outgoing)
        now, local, edge_local, *base = call(
            functools.partial(field_kernel, number),
            [field, field, edge_field] + [shape(vecs, vecs)] * (number == 2),
            [SM] + [VM] * 14,
            scratch_shapes=scratch,
        )(cols, live_counts, *arrived, local, stored, degree, place, back, own, bound if number else own, *earlier)
        earlier = [begin, now] if number == 0 else [now, now]
        arrived = coming

    gram = call(gram_kernel, shape(vecs // 2, LANES), [VM] * 8)(*arrived, edge_local, same, peak, *base)
    gram = spread(gram, jnp.add, stages[:1])
    if sizes == (8, 4):
        parts = all_of(total(all_of(gram, "gx", (4, 6, 2))), "gy", (3, 2, 1))
    else:
        parts = [spread(gram, jnp.add, stages[1:])]
    now = call(last_kernel, shape(3 * vecs, cells, dtype=BF16), [VM] * 7)(*arrived, local, back, peak)
    root = math.sqrt(cells * sizes[0] * sizes[1])
    return call(functools.partial(encode_kernel, root), shape(1, 1, vecs, cells), [VM] * (len(parts) + 1), scratch_shapes=[pltpu.VMEM((2, 8, 8, vecs), F32)])(
        *parts, now
    )


def solution(mesh):
    in_specs = (
        P("gx", "gy", None, None),
        P("gx", "gy", None, None, None, None),
        P("gx", "gy", None, None),
        P("gx", "gy", None, None),
        P("gx", "gy"),
    )
    out_specs = P("gx", "gy", None, None)

    return jax.shard_map(per_device, mesh=mesh, in_specs=in_specs, out_specs=out_specs, check_vma=False)
```
